256 devices in a mesh: ctx: 32 (over y, z), mp: 8 (over x, core).
Axes of the slice: x: 4, y: 4, z: 8, core: 2. Of those that a mesh axis runs over, the one named last changes fastest.
Arguments:
- tokens: bfloat16 [32768, 4096], P('ctx'), may hold values from -6 to 6
- lru_in_weight: bfloat16 [4096, 4096], P(None, 'mp'), may hold values from -0.09375 to 0.09375
- gelu_weight: bfloat16 [4096, 4096], P(None, 'mp'), may hold values from -0.09375 to 0.09375
- conv_weight: bfloat16 [4, 4096], P(None, 'mp'), may hold values from -3 to 3
- recur_gate_weight: bfloat16 [16, 256, 256], P('mp'), may hold values from -0.375 to 0.375
- input_gate_weight: bfloat16 [16, 256, 256], P('mp'), may hold values from -0.375 to 0.375
- decay_rate: float32 [4096], P('mp'), may hold values from 6.1035155e-07 to 0.02
- segment_pos: int32 [32768], P('ctx'), may hold values from 0 to 16895, as said below
- source_row: int32 [32768], P('ctx'), may hold values from 0 to 32767, as said below
Outputs:
- block_out: bfloat16 [32768, 4096], P(('ctx', 'mp'))
The draws below stay inside these ranges and needn't reach their ends.
Inputs may be any that keep to these rules, and one draw needn't show every extreme that they name: `source_row`: window position p belongs to context shard c = p // 1024. Every loader row appears once. Loader shard l sends to context shard c exactly the rows l * 1024 + c * 32 to l * 1024 + (c + 1) * 32 - 1. `segment_pos`: counts positions since the last document start; it rises by one except at document starts, where it is 0. The first document covers rows 0 to 16895; the other 7 documents start at row 16896 and at 6 further rows after it.
All inputs are finite; a program needn't handle non-finite values.
Results may differ from the reference program's by a relative error of at most 0.012.
Values may be sent and summed in bfloat16 or wider, within the bound.
A program may use at most 128 MiB of HBM per device.

```python
import math
import jax
import jax.numpy as jnp
from jax import lax

D = 4096
H = 16
BS = 256
CONV = 4
NDOCS = 8
TOK_DEV = 1024
TOKENS = 32768
W = 4096


def draw_segment_pos(key, part):
    start_row = TOKENS // 2 + TOK_DEV // 2
    cuts = jax.random.permutation(key, TOKENS - start_row - 1)[:NDOCS - 2].astype(jnp.int32) + start_row + 1
    starts = jnp.zeros((TOKENS,), jnp.int32).at[cuts].set(1).at[0].set(1).at[start_row].set(1)
    places = jnp.arange(TOKENS, dtype=jnp.int32)
    latest = lax.cummax(places * starts, axis=0)
    return places - latest


def draw_source_row(key, part):
    shard_count = TOKENS // TOK_DEV
    share_rows = TOK_DEV // shard_count
    keys = jax.random.split(key, shard_count)
    orders = jax.vmap(lambda one_key: jax.random.permutation(one_key, TOK_DEV))(keys).astype(jnp.int32)
    shard_ids = jnp.arange(shard_count, dtype=jnp.int32)[:, None]
    loader = orders // share_rows
    within = orders % share_rows
    return (loader * TOK_DEV + shard_ids * share_rows + within).reshape(TOKENS).astype(jnp.int32)


def block_levels(own_key, shape, cuts, low, top_value):
    def one(dim, parts):
        heights = jax.random.uniform(jax.random.fold_in(jax.random.fold_in(own_key, 6), dim), (parts,), jnp.float32, low / len(cuts), top_value / len(cuts))
        return jnp.repeat(jnp.exp(heights), shape[dim] // parts).reshape((-1,) + (1,) * (len(shape) - dim - 1))

    loudness = one(*cuts[0])
    for cut in cuts[1:]:
        loudness = loudness * one(*cut)
    return loudness


def normal_values(own_key, shape, spread, most, pieces=(), kind=jnp.bfloat16):
    array = spread * jax.random.normal(own_key, shape, jnp.float32)
    if pieces:
        array = array * block_levels(own_key, shape, pieces, -0.22, 0.18)
    return jnp.clip(array, -most, most).astype(kind)


def setup_inputs(seed: int = 0) -> dict:
    arg_keys = jax.random.split(jax.random.key(seed), 10)
    return {
        "tokens": normal_values(arg_keys[0], (TOKENS, D), 1.0, 6.0, ((0, 32),)),
        "lru_in_weight": normal_values(arg_keys[1], (D, W), D ** -0.5, 0.09375, ((1, 8),)),
        "gelu_weight": normal_values(arg_keys[2], (D, W), D ** -0.5, 0.09375, ((1, 8),)),
        "conv_weight": normal_values(arg_keys[3], (CONV, W), 0.5, 3.0, ((1, 8),)),
        "recur_gate_weight": normal_values(arg_keys[4], (H, BS, BS), BS ** -0.5, 0.375, ((0, 8),)),
        "input_gate_weight": normal_values(arg_keys[5], (H, BS, BS), BS ** -0.5, 0.375, ((0, 8),)),
        "decay_rate": jnp.clip(jnp.exp(math.log(0.02) - 10.3972077 * jax.random.uniform(arg_keys[6], (W,), jnp.float32) ** block_levels(arg_keys[6], (W,), ((0, 8),), -0.2, 0.2)), 6.103515488575795e-07, 0.02),
        "segment_pos": draw_segment_pos(jax.random.fold_in(arg_keys[9], 71), 0),
        "source_row": draw_source_row(jax.random.fold_in(arg_keys[9], 71), 0),
    }


def reference(tokens, lru_in_weight, gelu_weight, conv_weight, recur_gate_weight, input_gate_weight, decay_rate, segment_pos, source_row):
    window = tokens[source_row]
    branch = jnp.dot(window, lru_in_weight, preferred_element_type=jnp.float32).astype(jnp.bfloat16)
    gate_rows = jnp.dot(window, gelu_weight, preferred_element_type=jnp.float32).astype(jnp.bfloat16)
    branch_f = branch.astype(jnp.float32)
    conv_sum = jnp.zeros((TOKENS, H * BS), jnp.float32)
    for offset in range(CONV):
        shifted = jnp.pad(branch_f, ((offset, 0), (0, 0)))[:TOKENS]
        live_mask = (segment_pos >= offset).astype(jnp.float32)[:, None]
        conv_sum = conv_sum + conv_weight[offset].astype(jnp.float32)[None, :] * shifted * live_mask
    conv_out = conv_sum.astype(jnp.bfloat16)
    grouped = conv_out.astype(jnp.float32).reshape(TOKENS, H, BS)
    recur_gate = jax.nn.sigmoid(jnp.einsum('tkb,kbc->tkc', grouped, recur_gate_weight.astype(jnp.float32)).reshape(TOKENS, H * BS))
    input_gate = jax.nn.sigmoid(jnp.einsum('tkb,kbc->tkc', grouped, input_gate_weight.astype(jnp.float32)).reshape(TOKENS, H * BS))
    log_decay = -8.0 * recur_gate * decay_rate[None, :]
    decay_step = jnp.exp(log_decay)
    starts = (segment_pos == 0)[:, None]
    scale_in = jnp.where(starts, jnp.float32(1.0), jnp.sqrt(-jnp.expm1(2.0 * log_decay)))
    drive_term = scale_in * input_gate * conv_out.astype(jnp.float32)
    carried = jnp.where(starts, jnp.float32(0.0), decay_step)

    def advance(state_now, inputs):
        state_next = inputs[0] * state_now + inputs[1]
        return (state_next, state_next)
    _, full_state = lax.scan(advance, jnp.zeros((H * BS,), jnp.float32), (carried, drive_term))
    state_rows = lax.optimization_barrier(full_state.astype(jnp.bfloat16))
    window_out = (state_rows.astype(jnp.float32) * jax.nn.gelu(gate_rows.astype(jnp.float32), approximate=True)).astype(jnp.bfloat16)
    return jnp.zeros_like(window_out).at[source_row].set(window_out)
```

```python
import functools

import jax
import jax.numpy as jnp
from jax import lax
from jax.experimental import pallas as pl
from jax.experimental.pallas import tpu as pltpu
from jax.sharding import PartitionSpec as P

MESH = pl.DeviceIdType.MESH
ANY = pl.BlockSpec(memory_space=pl.ANY)
VMEM = pl.BlockSpec(memory_space=pltpu.VMEM)
BF = jnp.bfloat16
F32 = jnp.float32
SUB = 8
HEAD = 16
DOT = functools.partial(jnp.dot, preferred_element_type=F32)


def one_minus_exp_minus(v):
    poly = F32(1.0 / 40320.0)
    for order in (5040.0, 720.0, 120.0, 24.0, 6.0, 2.0, 1.0):
        poly = F32(1.0 / order) - v * poly
    return v * poly


def kernel(
    dims,
    tok_hbm,
    lru_hbm,
    gelu_hbm,
    conv_ref,
    recur_hbm,
    input_hbm,
    rate_ref,
    seg_ref,
    src_ref,
    out_hbm,
    tok,
    lru,
    gel,
    recw,
    inpw,
    seg_b,
    idx_b,
    perm,
    perm_t,
    send1,
    recv1,
    send2,
    recv2,
    gate,
    fin,
    orecv,
    win,
    conv,
    lin_r,
    lin_i,
    decay,
    state,
    ends,
    rim_s,
    rim_r,
    sum_s,
    sum_r,
    rows16,
    load_sem,
    out_sem,
    s1,
    r1,
    s2,
    r2,
    sm,
    rm,
    ss,
    rs,
    sr,
    rr,
):
    ny, nz, n_mp, blocks, bs = dims
    n_ctx = ny * nz
    rows_all, depth = tok.shape
    share = rows_all // n_ctx
    part = rows_all // ny
    seg_rows = rows_all // SUB
    mp_rows = rows_all // n_mp
    per_y = n_mp // ny
    c = lax.axis_index("ctx")
    m = lax.axis_index("mp")
    y, z, x = c // nz, lax.rem(c, nz), m // 2
    barrier = pltpu.get_barrier_semaphore()

    @pl.loop(1, n_ctx)
    def _(k):
        pl.semaphore_signal(
            barrier, inc=1, device_id={"ctx": lax.rem(c + k, n_ctx)}, device_id_type=MESH
        )

    @pl.loop(1, n_mp)
    def _(k):
        pl.semaphore_signal(
            barrier, inc=1, device_id={"mp": lax.rem(m + k, n_mp)}, device_id_type=MESH
        )

    def remote(src, dst, send_sem, recv_sem, **device):
        return pltpu.make_async_remote_copy(
            src_ref=src,
            dst_ref=dst,
            send_sem=send_sem,
            recv_sem=recv_sem,
            device_id=device,
            device_id_type=MESH,
        )

    def part_rows(k):
        return pl.ds(pl.multiple_of(lax.rem(y + k, ny) * part, part), part)

    def load_tok(k):
        return pltpu.make_async_copy(
            tok_hbm.at[part_rows(k)], tok.at[part_rows(k)], load_sem.at[k]
        )

    def load_w(hbm, buf, b, at):
        return pltpu.make_async_copy(
            hbm.at[:, b * bs : (b + 1) * bs], buf.at[b], load_sem.at[at]
        )

    at = ny
    lru_loads = [load_w(lru_hbm, lru, b, at + b) for b in range(blocks)]
    at += blocks
    gel_loads = [load_w(gelu_hbm, gel, b, at + b) for b in range(blocks)]
    at += blocks
    gate_loads = [
        pltpu.make_async_copy(recur_hbm, recw, load_sem.at[at]),
        pltpu.make_async_copy(input_hbm, inpw, load_sem.at[at + 1]),
    ]
    lru_loads[0].start()
    for k in range(ny):
        load_tok(k).start()
    for copy in lru_loads[1:] + gate_loads + gel_loads:
        copy.start()

    src = src_ref[...]
    idx = (src // rows_all) * share + lax.rem(src, rows_all) - c * share
    seg = seg_ref[...]
    for j in range(seg_rows):
        idx_b[j] = jnp.broadcast_to(idx[:, j : j + 1], (SUB, 128))
        seg_b[j] = jnp.broadcast_to(seg[:, j : j + 1], (SUB, 128))
    lanes = lax.broadcasted_iota(jnp.int32, (128, 128), 1)

    @pl.loop(0, rows_all // 128)
    def _(g):
        want = idx_b[pl.ds(g * 16, 16)].reshape(128, 128)
        here = pl.ds(pl.multiple_of(g * 128, 128), 128)
        for t in range(rows_all // 128):
            hot = jnp.where(want == lanes + t * 128, F32(1.0), F32(0.0))
            perm[here, t * 128 : (t + 1) * 128] = hot.astype(BF)
            perm_t[t * 128 : (t + 1) * 128, here] = hot.T.astype(BF)

    def project(b, k):
        rows = part_rows(k)
        branch = DOT(tok[rows, :], lru[b]).astype(BF)
        first = lax.rem(y + k, ny) * nz
        send1[b, pl.ds(first, nz)] = branch.reshape(nz, share, bs)

    def send_part(buf, into, b, k, s_sem, r_sem):
        first = lax.rem(y + k, ny) * nz
        for dz in range(nz):
            d = first + lax.rem(z + dz, nz)

            @pl.when(d != c)
            def _():
                remote(buf.at[b, d], into.at[b, c], s_sem.at[b, d], r_sem.at[b, c], ctx=d).start()

            @pl.when(d == c)
            def _():
                into[b, c] = buf[b, c]

    def gate_part(b, k):
        rows = part_rows(k)
        line = DOT(tok[rows, :], gel[b]).astype(BF).astype(F32)
        gate[b, rows, :] = jax.nn.gelu(line, approximate=True)

    lru_loads[0].wait()
    load_tok(0).wait()
    project(0, 0)
    pl.semaphore_wait(barrier, n_ctx + n_mp - 2)
    send_part(send1, recv1, 0, 0, s1, r1)

    @pl.loop(1, ny)
    def _(k):
        load_tok(k).wait()
        project(0, k)
        send_part(send1, recv1, 0, k, s1, r1)

    for b in range(1, blocks):
        lru_loads[b].wait()

        @pl.loop(0, ny)
        def _(k):
            project(b, k)
            send_part(send1, recv1, b, k, s1, r1)

    for copy in gate_loads + gel_loads:
        copy.wait()

    @pl.loop(0, ny)
    def _(k):
        gate_part(0, k)

    def wait_from(buf, b, sem, other_sem, source):
        @pl.when(source != c)
        def _():
            remote(buf.at[b, source], buf.at[b, source], other_sem.at[b, source], sem.at[b, source], ctx=source).wait_recv()

    lanes_bs = bs // 128

    def wide(v):
        return jnp.concatenate([v] * lanes_bs, axis=-1)

    def conv_range(b, j0, nj):
        taps = conv_ref[:, b * bs : (b + 1) * bs].astype(F32)
        pos = wide(seg_b[pl.ds(j0, nj)])
        total = taps[0:1, :] * win[pl.ds(j0 + 3, nj)]
        for k in range(1, 4):
            total = total + taps[k : k + 1, :] * jnp.where(
                pos >= k, win[pl.ds(j0 + 3 - k, nj)], F32(0.0)
            )
        conv[pl.ds(pl.multiple_of(j0 * SUB, SUB * nj), nj * SUB), :] = total.reshape(nj * SUB, bs).astype(BF)

    def gates_range(b, r0, nr):
        grouped = conv[r0 : r0 + nr, :]
        lin_r[r0 : r0 + nr, :] = DOT(grouped, recw[b])
        lin_i[r0 : r0 + nr, :] = DOT(grouped, inpw[b])

    def scan_range(b, j0, nj, carry):
        cum, now = carry
        rows = pl.ds(pl.multiple_of(j0 * SUB, SUB * nj), nj * SUB)
        rate8 = 8.0 * rate_ref[:, b * bs : (b + 1) * bs]
        rate_gate = jax.nn.sigmoid(lin_r[rows, :])
        in_gate = jax.nn.sigmoid(lin_i[rows, :])
        fall = rate_gate * rate8
        starts = wide(seg_b[pl.ds(j0, nj)]).reshape(nj * SUB, bs) == 0
        step = jnp.where(starts, F32(0.0), jnp.exp(-fall))
        scale = jnp.where(starts, F32(1.0), jnp.sqrt(one_minus_exp_minus(2.0 * fall)))
        drive = scale * in_gate * conv[rows, :].astype(F32)
        for j in range(nj):
            a = step[j * SUB : (j + 1) * SUB]
            now = a * now + drive[j * SUB : (j + 1) * SUB]
            cum = a * cum
            decay[b, j0 + j] = cum
            state[b, j0 + j] = now
        return cum, now

    fresh = (jnp.ones((SUB, bs), F32), jnp.zeros((SUB, bs), F32))
    step_j = 8

    def first_pass(b):
        @pl.loop(0, n_ctx)
        def _(source):
            wait_from(recv1, b, r1, s1, source)

        got = recv1[b].reshape(rows_all, bs)
        quarter = rows_all // 4
        for q in range(4):
            block = DOT(perm[q * quarter : (q + 1) * quarter, :], got)
            win[3 + q * quarter // SUB : 3 + (q + 1) * quarter // SUB] = block.reshape(quarter // SUB, SUB, bs)
        tails = [win[seg_rows + k, SUB - 1 : SUB, :] for k in range(3)]
        rim_s[b] = jnp.concatenate(tails + [jnp.zeros((SUB - 3, bs), F32)], axis=0)

        @pl.when(c < n_ctx - 1)
        def _():
            remote(rim_s.at[b], rim_r.at[b], sr.at[b], rr.at[b], ctx=c + 1).start()

        @pl.loop(HEAD // step_j, seg_rows // step_j)
        def _(g):
            conv_range(b, g * step_j, step_j)

        body = rows_all - HEAD * SUB
        half = body // 2 // 16 * 16
        gates_range(b, HEAD * SUB, half)
        gates_range(b, HEAD * SUB + half, body - half)
        cum, now = lax.fori_loop(
            HEAD // step_j,
            seg_rows // step_j,
            lambda g, carry: scan_range(b, g * step_j, step_j, carry),
            fresh,
        )
        ends[b, 2], ends[b, 3] = cum, now

    def second_pass(b):
        @pl.when(c == 0)
        def _():
            rim_r[b] = jnp.zeros((SUB, bs), F32)

        @pl.when(c > 0)
        def _():
            remote(rim_r.at[b], rim_r.at[b], sr.at[b], rr.at[b], ctx=c - 1).wait_recv()

        for k in range(3):
            win[k] = jnp.concatenate(
                [rim_r[b, k : k + 1, :], win[seg_rows + k, 0 : SUB - 1, :]], axis=0
            )
        for g in range(HEAD // step_j):
            conv_range(b, g * step_j, step_j)
        gates_range(b, 0, HEAD * SUB)
        carry = fresh
        for g in range(HEAD // step_j):
            carry = scan_range(b, g * step_j, step_j, carry)
        ends[b, 0], ends[b, 1] = carry
        cum, now = carry[0] * ends[b, 2], ends[b, 2] * carry[1] + ends[b, 3]
        ends[b, 4], ends[b, 5] = cum, now
        whole_c, whole_h = cum[0:1], now[0:1]
        for s in range(1, SUB):
            whole_h = cum[s : s + 1] * whole_h + now[s : s + 1]
            whole_c = cum[s : s + 1] * whole_c
        sum_s[b] = jnp.concatenate([whole_c, whole_h], axis=0)

        @pl.loop(c + 1, n_ctx)
        def _(d):
            remote(sum_s.at[b], sum_r.at[b, c], ss.at[b, d], rs.at[b, c], ctx=d).start()

    def third_pass(b):
        def join(source, incoming):
            remote(sum_r.at[b, source], sum_r.at[b, source], ss.at[b, source], rs.at[b, source], ctx=source).wait_recv()
            both = sum_r[b, source]
            return both[0:1] * incoming + both[1:2]

        incoming = lax.fori_loop(0, c, join, jnp.zeros((1, bs), F32))
        cum, now = ends[b, 4], ends[b, 5]
        lines = [incoming]
        for s in range(SUB - 1):
            lines.append(cum[s : s + 1] * lines[-1] + now[s : s + 1])
        head_in = jnp.concatenate(lines, axis=0)
        body_in = ends[b, 0] * head_in + ends[b, 1]

        def fix(g, into):
            j0 = g * step_j
            full = state[b, pl.ds(j0, step_j)] + decay[b, pl.ds(j0, step_j)] * into
            rows16[pl.ds(pl.multiple_of(j0 * SUB, step_j * SUB), step_j * SUB), :] = full.reshape(step_j * SUB, bs).astype(BF)
            return into

        for g in range(HEAD // step_j):
            fix(g, head_in)
        lax.fori_loop(HEAD // step_j, seg_rows // step_j, fix, body_in)

        @pl.loop(0, ny)
        def _(i):
            k = lax.rem(i + x, ny)
            block = DOT(perm_t[part_rows(k), :], rows16[...]).astype(BF)
            send2[b, pl.ds(lax.rem(y + k, ny) * nz, nz)] = block.reshape(nz, share, bs)
            send_part(send2, recv2, b, k, s2, r2)

    def finish(b):
        @pl.loop(0, ny)
        def _(i):
            other = lax.rem(y + 2 * ny - lax.rem(i + x, ny), ny)

            @pl.loop(0, nz)
            def _(k):
                wait_from(recv2, b, r2, s2, other * nz + k)

            for q in range(per_y):
                owner = other * per_y + q
                shares = mp_rows // share
                rows = pl.ds(pl.multiple_of(owner * mp_rows, mp_rows), mp_rows)
                got = recv2[b, pl.ds(owner * shares, shares)].reshape(mp_rows, bs)
                result = (got.astype(F32) * gate[b, rows, :]).astype(BF)

                @pl.when(owner == m)
                def _():
                    orecv[b, m] = result

                @pl.when(owner != m)
                def _():
                    fin[b, owner] = result
                    remote(fin.at[b, owner], orecv.at[b, m], sm.at[b, owner], rm.at[b, m], mp=owner).start()

    first_pass(0)
    second_pass(0)
    for b in range(1, blocks):
        first_pass(b)
        second_pass(b)
    for b in range(blocks):
        third_pass(b)
    for b in range(1, blocks):

        @pl.loop(0, ny)
        def _(k):
            gate_part(b, k)

    for b in range(blocks):
        finish(b)

    def out_copy(b, source):
        lane = pl.multiple_of(source * (blocks * bs) + b * bs, bs)
        return pltpu.make_async_copy(
            orecv.at[b, source], out_hbm.at[:, pl.ds(lane, bs)], out_sem.at[b, source]
        )

    for b in range(blocks):

        @pl.loop(0, n_mp)
        def _(source):
            @pl.when(source != m)
            def _():
                remote(orecv.at[b, source], orecv.at[b, source], sm.at[b, source], rm.at[b, source], mp=source).wait_recv()

            out_copy(b, source).start()

    for b in range(blocks):

        @pl.loop(0, n_ctx)
        def _(d):
            @pl.when(d != c)
            def _():
                remote(send1.at[b, d], recv1.at[b, c], s1.at[b, d], r1.at[b, c], ctx=d).wait_send()
                remote(send2.at[b, d], recv2.at[b, c], s2.at[b, d], r2.at[b, c], ctx=d).wait_send()

        @pl.loop(c + 1, n_ctx)
        def _(d):
            remote(sum_s.at[b], sum_r.at[b, c], ss.at[b, d], rs.at[b, c], ctx=d).wait_send()

        @pl.when(c < n_ctx - 1)
        def _():
            remote(rim_s.at[b], rim_r.at[b], sr.at[b], rr.at[b], ctx=c + 1).wait_send()

        @pl.loop(0, n_mp)
        def _(d):
            @pl.when(d != m)
            def _():
                remote(fin.at[b, d], orecv.at[b, m], sm.at[b, d], rm.at[b, m], mp=d).wait_send()

            out_copy(b, d).wait()


def body(ny, nz, n_mp, tokens, lru_w, gelu_w, conv_w, recur_w, input_w, rate, seg, src):
    rows_all, depth = tokens.shape
    width = lru_w.shape[1]
    blocks, bs = recur_w.shape[:2]
    n_ctx = ny * nz
    share, seg_rows, mp_rows = rows_all // n_ctx, rows_all // SUB, rows_all // n_mp
    dma = pltpu.SemaphoreType.DMA
    return pl.pallas_call(
        functools.partial(kernel, (ny, nz, n_mp, blocks, bs)),
        out_shape=jax.ShapeDtypeStruct((mp_rows, n_mp * width), BF),
        in_specs=[ANY, ANY, ANY, VMEM, ANY, ANY, VMEM, VMEM, VMEM],
        out_specs=ANY,
        scratch_shapes=[
            pltpu.VMEM((rows_all, depth), BF),
            pltpu.VMEM((blocks, depth, bs), BF),
            pltpu.VMEM((blocks, depth, bs), BF),
            pltpu.VMEM((blocks, bs, bs), BF),
            pltpu.VMEM((blocks, bs, bs), BF),
            pltpu.VMEM((seg_rows, SUB, 128), jnp.int32),
            pltpu.VMEM((seg_rows, SUB, 128), jnp.int32),
            pltpu.VMEM((rows_all, rows_all), BF),
            pltpu.VMEM((rows_all, rows_all), BF),
            pltpu.VMEM((blocks, n_ctx, share, bs), BF),
            pltpu.VMEM((blocks, n_ctx, share, bs), BF),
            pltpu.VMEM((blocks, n_ctx, share, bs), BF),
            pltpu.VMEM((blocks, n_ctx, share, bs), BF),
            pltpu.VMEM((blocks, rows_all, bs), F32),
            pltpu.VMEM((blocks, n_mp, mp_rows, bs), BF),
            pltpu.VMEM((blocks, n_mp, mp_rows, bs), BF),
            pltpu.VMEM((seg_rows + 3, SUB, bs), F32),
            pltpu.VMEM((rows_all, bs), BF),
            pltpu.VMEM((rows_all, bs), F32),
            pltpu.VMEM((rows_all, bs), F32),
            pltpu.VMEM((blocks, seg_rows, SUB, bs), F32),
            pltpu.VMEM((blocks, seg_rows, SUB, bs), F32),
            pltpu.VMEM((blocks, 6, SUB, bs), F32),
            pltpu.VMEM((blocks, SUB, bs), F32),
            pltpu.VMEM((blocks, SUB, bs), F32),
            pltpu.VMEM((blocks, 2, bs), F32),
            pltpu.VMEM((blocks, n_ctx, 2, bs), F32),
            pltpu.VMEM((rows_all, bs), BF),
            dma((ny + 2 * blocks + 2,)),
            dma((blocks, n_mp)),
            dma((blocks, n_ctx)),
            dma((blocks, n_ctx)),
            dma((blocks, n_ctx)),
            dma((blocks, n_ctx)),
            dma((blocks, n_mp)),
            dma((blocks, n_mp)),
            dma((blocks, n_ctx)),
            dma((blocks, n_ctx)),
            dma((blocks,)),
            dma((blocks,)),
        ],
        compiler_params=pltpu.CompilerParams(
            collective_id=0, has_side_effects=True, vmem_limit_bytes=60 * 1024 * 1024
        ),
    )(
        tokens,
        lru_w,
        gelu_w,
        conv_w,
        recur_w,
        input_w,
        rate.reshape(1, width),
        seg.reshape(SUB, seg_rows),
        src.reshape(SUB, seg_rows),
    )


def solution(mesh, ny=None):
    n_ctx, n_mp = mesh.shape["ctx"], mesh.shape["mp"]
    ny = ny or 4
    in_specs = (
        P("ctx", None),
        P(None, "mp"),
        P(None, "mp"),
        P(None, "mp"),
        P("mp", None, None),
        P("mp", None, None),
        P("mp"),
        P("ctx"),
        P("ctx"),
    )
    out_specs = P(("ctx", "mp"), None)
    return jax.shard_map(
        functools.partial(body, ny, n_ctx // ny, n_mp),
        mesh=mesh,
        in_specs=in_specs,
        out_specs=out_specs,
        check_vma=False,
    )
```

```python
import functools

import jax
import jax.numpy as jnp
from jax import lax
from jax.experimental import pallas as pl
from jax.experimental.pallas import tpu as pltpu
from jax.sharding import PartitionSpec as P

MESH = pl.DeviceIdType.MESH
ANY = pl.BlockSpec(memory_space=pl.ANY)
VMEM = pl.BlockSpec(memory_space=pltpu.VMEM)
BF = jnp.bfloat16
F32 = jnp.float32
SUB = 8
HEAD = 16
WINDOW = 10
DOT = functools.partial(jnp.dot, preferred_element_type=F32)


def one_minus_exp_minus(v):
    poly = F32(1.0 / 40320.0)
    for order in (5040.0, 720.0, 120.0, 24.0, 6.0, 2.0, 1.0):
        poly = F32(1.0 / order) - v * poly
    return v * poly


def kernel(
    dims,
    tok_hbm,
    lru_hbm,
    gelu_hbm,
    conv_ref,
    recur_hbm,
    input_hbm,
    rate_ref,
    seg_ref,
    src_ref,
    out_hbm,
    tok,
    lru,
    gel,
    recw,
    inpw,
    seg_b,
    idx_b,
    perm,
    perm_t,
    send1,
    recv1,
    send2,
    recv2,
    gate,
    fin,
    orecv,
    win,
    conv,
    lin_r,
    lin_i,
    decay,
    state,
    ends,
    rim_s,
    rim_r,
    sum_s,
    sum_r,
    rows16,
    load_sem,
    out_sem,
    s1,
    r1,
    w1,
    s2,
    r2,
    w2,
    sm,
    rm,
    ss,
    rs,
    sr,
    rr,
):
    ny, nz, n_mp, blocks, bs = dims
    n_ctx = ny * nz
    window = w1.shape[0]
    rows_all, depth = tok.shape
    share = rows_all // n_ctx
    part = rows_all // ny
    seg_rows = rows_all // SUB
    mp_rows = rows_all // n_mp
    per_y = n_mp // ny
    c = lax.axis_index("ctx")
    m = lax.axis_index("mp")
    y, z, x = c // nz, lax.rem(c, nz), m // 2
    barrier = pltpu.get_barrier_semaphore()

    @pl.loop(1, n_ctx)
    def _(k):
        pl.semaphore_signal(
            barrier, inc=1, device_id={"ctx": lax.rem(c + k, n_ctx)}, device_id_type=MESH
        )

    @pl.loop(1, n_mp)
    def _(k):
        pl.semaphore_signal(
            barrier, inc=1, device_id={"mp": lax.rem(m + k, n_mp)}, device_id_type=MESH
        )

    def remote(src, dst, send_sem, recv_sem, **device):
        return pltpu.make_async_remote_copy(
            src_ref=src,
            dst_ref=dst,
            send_sem=send_sem,
            recv_sem=recv_sem,
            device_id=device,
            device_id_type=MESH,
        )

    def part_rows(k):
        return pl.ds(pl.multiple_of(lax.rem(y + k, ny) * part, part), part)

    def load_tok(k):
        return pltpu.make_async_copy(
            tok_hbm.at[part_rows(k)], tok.at[part_rows(k)], load_sem.at[k]
        )

    def load_w(hbm, buf, b, at):
        return pltpu.make_async_copy(
            hbm.at[:, b * bs : (b + 1) * bs], buf.at[b], load_sem.at[at]
        )

    at = ny
    lru_loads = [load_w(lru_hbm, lru, b, at + b) for b in range(blocks)]
    at += blocks
    gel_loads = [load_w(gelu_hbm, gel, b, at + b) for b in range(blocks)]
    at += blocks
    gate_loads = [
        pltpu.make_async_copy(recur_hbm, recw, load_sem.at[at]),
        pltpu.make_async_copy(input_hbm, inpw, load_sem.at[at + 1]),
    ]
    lru_loads[0].start()
    for k in range(ny):
        load_tok(k).start()
    for copy in lru_loads[1:] + gate_loads + gel_loads:
        copy.start()

    def project(b, k):
        rows = part_rows(k)
        branch = DOT(tok[rows, :], lru[b]).astype(BF)
        first = lax.rem(y + k, ny) * nz
        send1[b, pl.ds(first, nz)] = branch.reshape(nz, share, bs)

    per_group = mp_rows // share
    group = c // per_group
    zg = z // per_group

    def target(t, turn):
        k = lax.rem(t // nz + turn, ny)
        q, e = lax.rem(t, nz) // per_group, lax.rem(t, per_group)
        to_y, to_g = lax.rem(y + k, ny), lax.rem(zg + q, per_y)
        return to_y * nz + to_g * per_group + lax.rem(z + e, per_group)

    def send_one(buf, into, b, t, turn, s_sem, r_sem):
        d = target(t, turn)

        @pl.when(d != c)
        def _():
            remote(buf.at[b, d], into.at[b, c], s_sem, r_sem, ctx=d).start()

        @pl.when(d == c)
        def _():
            into[b, c] = buf[b, c]

    def send_part(buf, into, b, i, turn, s_sem, r_sem):
        for e in range(nz):
            send_one(buf, into, b, i * nz + e, turn, s_sem, r_sem)

    def window_wait(buf, b, t, turn, slots):
        d = target(t, turn)

        @pl.when(d != c)
        def _():
            remote(buf.at[b, d], buf.at[b, d], slots.at[lax.rem(t, window)], slots.at[lax.rem(t, window)], ctx=d).wait_send()

    def pump(buf, into, b, turn, slots, r_sem):
        done = [0]

        def more(count):
            first = done[0]
            last = min(first + count, n_ctx)
            done[0] = last

            @pl.loop(first, last)
            def _(t):
                @pl.when(t >= window)
                def _():
                    window_wait(buf, b, t - window, turn, slots)

                send_one(buf, into, b, t, turn, slots.at[lax.rem(t, window)], r_sem)

        return more

    def window_end(buf, b, turn, slots):
        @pl.loop(n_ctx - window, n_ctx)
        def _(t):
            window_wait(buf, b, t, turn, slots)

    def build_perm():
        src = src_ref[...]
        idx = (src // rows_all) * share + lax.rem(src, rows_all) - c * share
        seg = seg_ref[...]
        for j in range(seg_rows):
            idx_b[j] = jnp.broadcast_to(idx[:, j : j + 1], (SUB, 128))
            seg_b[j] = jnp.broadcast_to(seg[:, j : j + 1], (SUB, 128))
        lanes = lax.broadcasted_iota(jnp.int32, (128, 128), 1)

        @pl.loop(0, rows_all // 128)
        def _(g):
            want = idx_b[pl.ds(g * 16, 16)].reshape(128, 128)
            here = pl.ds(pl.multiple_of(g * 128, 128), 128)
            for t in range(rows_all // 128):
                hot = jnp.where(want == lanes + t * 128, F32(1.0), F32(0.0))
                perm[here, t * 128 : (t + 1) * 128] = hot.astype(BF)
                perm_t[t * 128 : (t + 1) * 128, here] = hot.T.astype(BF)

    def gate_part(b, k):
        rows = part_rows(k)
        line = DOT(tok[rows, :], gel[b]).astype(BF).astype(F32)
        gate[b, rows, :] = jax.nn.gelu(line, approximate=True)

    lru_loads[0].wait()
    load_tok(0).wait()
    project(0, 0)
    with jax.named_scope("barrier"):
        pl.semaphore_wait(barrier, n_ctx + n_mp - 2)
    send_part(send1, recv1, 0, 0, 0, s1, r1.at[0])

    @pl.loop(1, ny)
    def _(k):
        load_tok(k).wait()
        project(0, k)
        send_part(send1, recv1, 0, k, 0, s1, r1.at[0])

    lru_loads[1].wait()

    @pl.loop(0, ny)
    def _(k):
        project(1, k)

    with jax.named_scope("perm"):
        build_perm()
    for copy in gate_loads + gel_loads:
        copy.wait()

    @pl.loop(0, ny)
    def _(k):
        gate_part(0, k)

    def got_all(ref, sem):
        remote(ref, ref, sem, sem, ctx=lax.rem(c + 1, n_ctx)).wait_recv()

    def sent_all(ref, sem):
        remote(ref, ref, sem, sem, ctx=lax.rem(c + 1, n_ctx)).wait_send()

    lanes_bs = bs // 128

    def wide(v):
        return jnp.concatenate([v] * lanes_bs, axis=-1)

    def conv_range(b, j0, nj):
        taps = conv_ref[:, b * bs : (b + 1) * bs].astype(F32)
        pos = wide(seg_b[pl.ds(j0, nj)])
        total = taps[0:1, :] * win[pl.ds(j0 + 3, nj)]
        for k in range(1, 4):
            total = total + taps[k : k + 1, :] * jnp.where(
                pos >= k, win[pl.ds(j0 + 3 - k, nj)], F32(0.0)
            )
        conv[pl.ds(pl.multiple_of(j0 * SUB, SUB * nj), nj * SUB), :] = total.reshape(nj * SUB, bs).astype(BF)

    def gates_range(b, r0, nr):
        grouped = conv[r0 : r0 + nr, :]
        lin_r[r0 : r0 + nr, :] = DOT(grouped, recw[b])
        lin_i[r0 : r0 + nr, :] = DOT(grouped, inpw[b])

    def scan_range(b, j0, nj, carry):
        cum, now = carry
        rows = pl.ds(pl.multiple_of(j0 * SUB, SUB * nj), nj * SUB)
        rate8 = 8.0 * rate_ref[:, b * bs : (b + 1) * bs]
        rate_gate = jax.nn.sigmoid(lin_r[rows, :])
        in_gate = jax.nn.sigmoid(lin_i[rows, :])
        fall = rate_gate * rate8
        starts = wide(seg_b[pl.ds(j0, nj)]).reshape(nj * SUB, bs) == 0
        step = jnp.where(starts, F32(0.0), jnp.exp(-fall))
        scale = jnp.where(starts, F32(1.0), jnp.sqrt(one_minus_exp_minus(2.0 * fall)))
        drive = scale * in_gate * conv[rows, :].astype(F32)
        for j in range(nj):
            a = step[j * SUB : (j + 1) * SUB]
            now = a * now + drive[j * SUB : (j + 1) * SUB]
            cum = a * cum
            decay[b, j0 + j] = cum
            state[b, j0 + j] = now
        return cum, now

    fresh = (jnp.ones((SUB, bs), F32), jnp.zeros((SUB, bs), F32))
    step_j = 8

    def first_pass(b, more):
        with jax.named_scope("wait1"):
            got_all(recv1.at[b, pl.ds(0, n_ctx - 1)], r1.at[b])
        got = recv1[b].reshape(rows_all, bs)
        quarter = rows_all // 4

        def permute(q):
            block = DOT(perm[q * quarter : (q + 1) * quarter, :], got)
            win[3 + q * quarter // SUB : 3 + (q + 1) * quarter // SUB] = block.reshape(quarter // SUB, SUB, bs)

        permute(3)
        tails = [win[seg_rows + k, SUB - 1 : SUB, :] for k in range(3)]
        rim_s[b] = jnp.concatenate(tails + [jnp.zeros((SUB - 3, bs), F32)], axis=0)

        @pl.when(c < n_ctx - 1)
        def _():
            remote(rim_s.at[b], rim_r.at[b], sr.at[b], rr.at[b], ctx=c + 1).start()

        for q in range(3):
            more(1)
            permute(q)
        more(1)

        @pl.loop(HEAD // step_j, seg_rows // step_j)
        def _(g):
            conv_range(b, g * step_j, step_j)

        body = rows_all - HEAD * SUB
        half = body // 2 // 16 * 16
        more(1)
        gates_range(b, HEAD * SUB, half)
        gates_range(b, HEAD * SUB + half, body - half)
        carry = fresh
        cuts = (HEAD // step_j, seg_rows // step_j // 2, seg_rows // step_j)
        for low, high in zip(cuts, cuts[1:]):
            more(2)
            carry = lax.fori_loop(
                low, high, lambda g, was: scan_range(b, g * step_j, step_j, was), carry
            )
        cum, now = carry
        more(2)
        ends[b, 2], ends[b, 3] = cum, now

    def second_pass(b):
        @pl.when(c == 0)
        def _():
            rim_r[b] = jnp.zeros((SUB, bs), F32)

        @pl.when(c > 0)
        def _():
            with jax.named_scope("waitrim"):
                got_all(rim_r.at[b], rr.at[b])

        for k in range(3):
            win[k] = jnp.concatenate(
                [rim_r[b, k : k + 1, :], win[seg_rows + k, 0 : SUB - 1, :]], axis=0
            )
        for g in range(HEAD // step_j):
            conv_range(b, g * step_j, step_j)
        gates_range(b, 0, HEAD * SUB)
        carry = fresh
        for g in range(HEAD // step_j):
            carry = scan_range(b, g * step_j, step_j, carry)
        ends[b, 0], ends[b, 1] = carry
        cum, now = carry[0] * ends[b, 2], ends[b, 2] * carry[1] + ends[b, 3]
        ends[b, 4], ends[b, 5] = cum, now
        whole_c, whole_h = cum[0:1], now[0:1]
        for s in range(1, SUB):
            whole_h = cum[s : s + 1] * whole_h + now[s : s + 1]
            whole_c = cum[s : s + 1] * whole_c
        sum_s[b] = jnp.concatenate([whole_c, whole_h], axis=0)

        @pl.loop(y + 1, ny)
        def _(to_y):
            for to_z in range(nz):
                remote(sum_s.at[b], sum_r.at[b, c], ss.at[b, to_y], rs.at[b, y], ctx=to_y * nz + to_z).start()

        @pl.loop(z + 1, nz)
        def _(to_z):
            remote(sum_s.at[b], sum_r.at[b, c], ss.at[b, ny + to_z], rs.at[b, ny + z], ctx=y * nz + to_z).start()

    def third_pass(b, send):
        def join(source, incoming):
            both = sum_r[b, source]
            return both[0:1] * incoming + both[1:2]

        def join_row(from_y, incoming):
            got_all(sum_r.at[b, pl.ds(from_y * nz, nz)], rs.at[b, from_y])
            for from_z in range(nz):
                incoming = join(from_y * nz + from_z, incoming)
            return incoming

        def join_own(from_z, incoming):
            got_all(sum_r.at[b, y * nz + from_z], rs.at[b, ny + from_z])
            return join(y * nz + from_z, incoming)

        with jax.named_scope("waitsum"):
            incoming = lax.fori_loop(0, y, join_row, jnp.zeros((1, bs), F32))
            incoming = lax.fori_loop(0, z, join_own, incoming)
        cum, now = ends[b, 4], ends[b, 5]
        lines = [incoming]
        for s in range(SUB - 1):
            lines.append(cum[s : s + 1] * lines[-1] + now[s : s + 1])
        head_in = jnp.concatenate(lines, axis=0)
        body_in = ends[b, 0] * head_in + ends[b, 1]

        def fix(g, into):
            j0 = g * step_j
            full = state[b, pl.ds(j0, step_j)] + decay[b, pl.ds(j0, step_j)] * into
            rows16[pl.ds(pl.multiple_of(j0 * SUB, step_j * SUB), step_j * SUB), :] = full.reshape(step_j * SUB, bs).astype(BF)
            return into

        for g in range(HEAD // step_j):
            fix(g, head_in)
        lax.fori_loop(HEAD // step_j, seg_rows // step_j, fix, body_in)

        @pl.loop(0, ny)
        def _(i):
            k = lax.rem(i + x, ny)
            block = DOT(perm_t[part_rows(k), :], rows16[...]).astype(BF)
            send2[b, pl.ds(lax.rem(y + k, ny) * nz, nz)] = block.reshape(nz, share, bs)
            if send:
                send_part(send2, recv2, b, i, x, s2, r2.at[b, group])

    def finish(b):
        @pl.loop(0, ny)
        def _(i):
            other = lax.rem(y + 2 * ny - lax.rem(i + x, ny), ny)
            for q in range(per_y):
                owner = other * per_y + lax.rem(zg + per_y - q, per_y)

                @pl.when(owner == group)
                def _():
                    got_all(recv2.at[b, pl.ds(0, per_group - 1)], r2.at[b, owner])

                @pl.when(owner != group)
                def _():
                    got_all(recv2.at[b, pl.ds(0, per_group)], r2.at[b, owner])

                rows = pl.ds(pl.multiple_of(owner * mp_rows, mp_rows), mp_rows)
                got = recv2[b, pl.ds(owner * per_group, per_group)].reshape(mp_rows, bs)
                result = (got.astype(F32) * gate[b, rows, :]).astype(BF)

                @pl.when(owner == m)
                def _():
                    orecv[b, m] = result

                @pl.when(owner != m)
                def _():
                    fin[b, owner] = result
                    remote(fin.at[b, owner], orecv.at[b, m], sm.at[b], rm.at[b], mp=owner).start()

    scope = jax.named_scope
    more = pump(send1, recv1, 1, 0, w1, r1.at[1])
    with scope("sent0"):
        sent_all(send1.at[0, pl.ds(0, n_ctx - 1)], s1)
        more(window)
    with scope("first0"):
        first_pass(0, more)
    with scope("second0"):
        second_pass(0)
    with scope("more0"):
        more(n_ctx)
    with scope("third0"):
        third_pass(0, False)
        more = pump(send2, recv2, 0, x, w2, r2.at[0, group])
        more(window)
    with scope("first1"):
        first_pass(1, more)
    with scope("second1"):
        second_pass(1)
    with scope("more1"):
        more(n_ctx)
    with scope("third1"):
        third_pass(1, True)

    with scope("gate1"):

        @pl.loop(0, ny)
        def _(k):
            gate_part(1, k)

    for b in range(blocks):
        with scope("finish"):
            finish(b)

    def out_copy(b, source):
        lane = pl.multiple_of(source * (blocks * bs) + b * bs, bs)
        return pltpu.make_async_copy(
            orecv.at[b, source], out_hbm.at[:, pl.ds(lane, bs)], out_sem.at[b, source]
        )

    with scope("drain"):
        window_end(send1, 1, 0, w1)
    window_end(send2, 0, x, w2)
    sent_all(send2.at[1, pl.ds(0, n_ctx - 1)], s2)
    for b in range(blocks):

        @pl.loop(y + 1, ny)
        def _(to_y):
            sent_all(sum_r.at[b, pl.ds(0, nz)], ss.at[b, to_y])

        @pl.loop(z + 1, nz)
        def _(to_z):
            sent_all(sum_s.at[b], ss.at[b, ny + to_z])

        @pl.when(c < n_ctx - 1)
        def _():
            sent_all(rim_s.at[b], sr.at[b])

        sent_all(fin.at[b, pl.ds(0, n_mp - 1)], sm.at[b])

    for b in range(blocks):
        with jax.named_scope("waitmp"):
            got_all(orecv.at[b, pl.ds(0, n_mp - 1)], rm.at[b])
        for source in range(n_mp):
            out_copy(b, source).start()
    with jax.named_scope("waitout"):
        for b in range(blocks):
            for source in range(n_mp):
                out_copy(b, source).wait()


def body(ny, nz, n_mp, tokens, lru_w, gelu_w, conv_w, recur_w, input_w, rate, seg, src):
    rows_all, depth = tokens.shape
    width = lru_w.shape[1]
    blocks, bs = recur_w.shape[:2]
    n_ctx = ny * nz
    share, seg_rows, mp_rows = rows_all // n_ctx, rows_all // SUB, rows_all // n_mp
    dma = pltpu.SemaphoreType.DMA
    return pl.pallas_call(
        functools.partial(kernel, (ny, nz, n_mp, blocks, bs)),
        out_shape=jax.ShapeDtypeStruct((mp_rows, n_mp * width), BF),
        in_specs=[ANY, ANY, ANY, VMEM, ANY, ANY, VMEM, VMEM, VMEM],
        out_specs=ANY,
        scratch_shapes=[
            pltpu.VMEM((rows_all, depth), BF),
            pltpu.VMEM((blocks, depth, bs), BF),
            pltpu.VMEM((blocks, depth, bs), BF),
            pltpu.VMEM((blocks, bs, bs), BF),
            pltpu.VMEM((blocks, bs, bs), BF),
            pltpu.VMEM((seg_rows, SUB, 128), jnp.int32),
            pltpu.VMEM((seg_rows, SUB, 128), jnp.int32),
            pltpu.VMEM((rows_all, rows_all), BF),
            pltpu.VMEM((rows_all, rows_all), BF),
            pltpu.VMEM((blocks, n_ctx, share, bs), BF),
            pltpu.VMEM((blocks, n_ctx, share, bs), BF),
            pltpu.VMEM((blocks, n_ctx, share, bs), BF),
            pltpu.VMEM((blocks, n_ctx, share, bs), BF),
            pltpu.VMEM((blocks, rows_all, bs), F32),
            pltpu.VMEM((blocks, n_mp, mp_rows, bs), BF),
            pltpu.VMEM((blocks, n_mp, mp_rows, bs), BF),
            pltpu.VMEM((seg_rows + 3, SUB, bs), F32),
            pltpu.VMEM((rows_all, bs), BF),
            pltpu.VMEM((rows_all, bs), F32),
            pltpu.VMEM((rows_all, bs), F32),
            pltpu.VMEM((blocks, seg_rows, SUB, bs), F32),
            pltpu.VMEM((blocks, seg_rows, SUB, bs), F32),
            pltpu.VMEM((blocks, 6, SUB, bs), F32),
            pltpu.VMEM((blocks, SUB, bs), F32),
            pltpu.VMEM((blocks, SUB, bs), F32),
            pltpu.VMEM((blocks, 2, bs), F32),
            pltpu.VMEM((blocks, n_ctx, 2, bs), F32),
            pltpu.VMEM((rows_all, bs), BF),
            dma((ny + 2 * blocks + 2,)),
            dma((blocks, n_mp)),
            dma,
            dma((blocks,)),
            dma((min(WINDOW, n_ctx // 2),)),
            dma,
            dma((blocks, n_mp)),
            dma((min(WINDOW, n_ctx // 2),)),
            dma((blocks,)),
            dma((blocks,)),
            dma((blocks, ny + nz)),
            dma((blocks, ny + nz)),
            dma((blocks,)),
            dma((blocks,)),
        ],
        compiler_params=pltpu.CompilerParams(
            collective_id=0, has_side_effects=True, vmem_limit_bytes=60 * 1024 * 1024
        ),
    )(
        tokens,
        lru_w,
        gelu_w,
        conv_w,
        recur_w,
        input_w,
        rate.reshape(1, width),
        seg.reshape(SUB, seg_rows),
        src.reshape(SUB, seg_rows),
    )


def solution(mesh, ny=None):
    n_ctx, n_mp = mesh.shape["ctx"], mesh.shape["mp"]
    ny = ny or 4
    in_specs = (
        P("ctx", None),
        P(None, "mp"),
        P(None, "mp"),
        P(None, "mp"),
        P("mp", None, None),
        P("mp", None, None),
        P("mp"),
        P("ctx"),
        P("ctx"),
    )
    out_specs = P(("ctx", "mp"), None)
    return jax.shard_map(
        functools.partial(body, ny, n_ctx // ny, n_mp),
        mesh=mesh,
        in_specs=in_specs,
        out_specs=out_specs,
        check_vma=False,
    )
```

```python
import functools

import jax
import jax.numpy as jnp
from jax import lax
from jax.experimental import pallas as pl
from jax.experimental.pallas import tpu as pltpu
from jax.sharding import PartitionSpec as P

MESH = pl.DeviceIdType.MESH
ANY = pl.BlockSpec(memory_space=pl.ANY)
VMEM = pl.BlockSpec(memory_space=pltpu.VMEM)
BF = jnp.bfloat16
F32 = jnp.float32
SUB = 8
HEAD = 16
WINDOW = 8
DOT = functools.partial(jnp.dot, preferred_element_type=F32)


def one_minus_exp_minus(v):
    poly = F32(1.0 / 40320.0)
    for order in (5040.0, 720.0, 120.0, 24.0, 6.0, 2.0, 1.0):
        poly = F32(1.0 / order) - v * poly
    return v * poly


def kernel(
    dims,
    tok_hbm,
    lru_hbm,
    gelu_hbm,
    conv_ref,
    recur_hbm,
    input_hbm,
    rate_ref,
    seg_ref,
    src_ref,
    out_hbm,
    tok,
    lru,
    gel,
    recw,
    inpw,
    seg_b,
    idx_b,
    perm,
    perm_t,
    send1,
    recv1,
    send2,
    recv2,
    gate,
    fin,
    orecv,
    win,
    conv,
    lin_r,
    lin_i,
    decay,
    state,
    ends,
    rim_s,
    rim_r,
    sum_s,
    sum_r,
    rows16,
    load_sem,
    out_sem,
    s1,
    r1,
    w1,
    s2,
    r2,
    w2,
    sm,
    rm,
    ss,
    rs,
    sr,
    rr,
):
    ny, nz, n_mp, blocks, bs = dims
    n_ctx = ny * nz
    window = w1.shape[0]
    rows_all, depth = tok.shape
    share = rows_all // n_ctx
    part = rows_all // ny
    seg_rows = rows_all // SUB
    mp_rows = rows_all // n_mp
    per_y = n_mp // ny
    c = lax.axis_index("ctx")
    m = lax.axis_index("mp")
    y, z, x = c // nz, lax.rem(c, nz), m // 2

    def low(v, size):
        return v & (size - 1)

    def high(v, size):
        return lax.shift_right_logical(v, size.bit_length() - 1)

    barrier = pltpu.get_barrier_semaphore()

    @pl.loop(1, n_ctx)
    def _(k):
        pl.semaphore_signal(
            barrier, inc=1, device_id={"ctx": lax.rem(c + k, n_ctx)}, device_id_type=MESH
        )

    @pl.loop(1, n_mp)
    def _(k):
        pl.semaphore_signal(
            barrier, inc=1, device_id={"mp": lax.rem(m + k, n_mp)}, device_id_type=MESH
        )

    def remote(src, dst, send_sem, recv_sem, **device):
        return pltpu.make_async_remote_copy(
            src_ref=src,
            dst_ref=dst,
            send_sem=send_sem,
            recv_sem=recv_sem,
            device_id=device,
            device_id_type=MESH,
        )

    def part_rows(k):
        return pl.ds(pl.multiple_of(low(y + k, ny) * part, part), part)

    def load_tok(k):
        return pltpu.make_async_copy(
            tok_hbm.at[part_rows(k)], tok.at[part_rows(k)], load_sem.at[k]
        )

    def load_w(hbm, buf, b, at):
        return pltpu.make_async_copy(
            hbm.at[:, b * bs : (b + 1) * bs], buf.at[b], load_sem.at[at]
        )

    at = ny
    lru_loads = [load_w(lru_hbm, lru, b, at + b) for b in range(blocks)]
    at += blocks
    gel_loads = [load_w(gelu_hbm, gel, b, at + b) for b in range(blocks)]
    at += blocks
    gate_loads = [
        pltpu.make_async_copy(recur_hbm, recw, load_sem.at[at]),
        pltpu.make_async_copy(input_hbm, inpw, load_sem.at[at + 1]),
    ]
    lru_loads[0].start()
    for k in range(ny):
        load_tok(k).start()
    for copy in lru_loads[1:] + gate_loads + gel_loads:
        copy.start()

    def project(b, k):
        rows = part_rows(k)
        branch = DOT(tok[rows, :], lru[b]).astype(BF)
        first = low(y + k, ny) * nz
        send1[b, pl.ds(first, nz)] = branch.reshape(nz, share, bs)

    per_group = mp_rows // share
    group = c // per_group
    zg = z // per_group

    def target(t, turn):
        to_y = low(y + high(t, nz) + turn, ny)
        to_g = low(zg + high(t, per_group), per_y)
        return to_y * nz + to_g * per_group + low(z + t, per_group)

    def send_one(buf, into, b, t, turn, s_sem, r_sem):
        d = target(t, turn)

        @pl.when(d != c)
        def _():
            remote(buf.at[b, d], into.at[b, c], s_sem, r_sem, ctx=d).start()

        @pl.when(d == c)
        def _():
            into[b, c] = buf[b, c]

    def send_part(buf, into, b, i, turn, s_sem, r_sem):
        for e in range(nz):
            send_one(buf, into, b, jnp.int32(i * nz + e), turn, s_sem, r_sem)

    def window_wait(buf, b, t, turn, slots):
        d = target(t, turn)

        @pl.when(d != c)
        def _():
            remote(buf.at[b, d], buf.at[b, d], slots.at[low(t, window)], slots.at[low(t, window)], ctx=d).wait_send()

    def pump(buf, into, b, turn, slots, r_sem):
        done = [0]

        def more(count):
            first = done[0]
            last = min(first + count, n_ctx)
            done[0] = last

            @pl.loop(first, last)
            def _(t):
                @pl.when(t >= window)
                def _():
                    window_wait(buf, b, t - window, turn, slots)

                send_one(buf, into, b, t, turn, slots.at[low(t, window)], r_sem)

        return more

    def window_end(buf, b, turn, slots):
        @pl.loop(n_ctx - window, n_ctx)
        def _(t):
            window_wait(buf, b, t, turn, slots)

    def build_perm():
        src = src_ref[...]
        idx = (src // rows_all) * share + lax.rem(src, rows_all) - c * share
        seg = seg_ref[...]
        for j in range(seg_rows):
            idx_b[j] = jnp.broadcast_to(idx[:, j : j + 1], (SUB, 128))
            seg_b[j] = jnp.broadcast_to(seg[:, j : j + 1], (SUB, 128))
        lanes = lax.broadcasted_iota(jnp.int32, (128, 128), 1)

        @pl.loop(0, rows_all // 128)
        def _(g):
            want = idx_b[pl.ds(g * 16, 16)].reshape(128, 128)
            here = pl.ds(pl.multiple_of(g * 128, 128), 128)
            for t in range(rows_all // 128):
                hot = jnp.where(want == lanes + t * 128, F32(1.0), F32(0.0))
                perm[here, t * 128 : (t + 1) * 128] = hot.astype(BF)
                perm_t[t * 128 : (t + 1) * 128, here] = hot.T.astype(BF)

    def gate_part(b, k):
        rows = part_rows(k)
        line = DOT(tok[rows, :], gel[b]).astype(BF).astype(F32)
        gate[b, rows, :] = jax.nn.gelu(line, approximate=True)

    lru_loads[0].wait()
    load_tok(0).wait()
    project(0, 0)
    with jax.named_scope("barrier"):
        pl.semaphore_wait(barrier, n_ctx + n_mp - 2)
    send_part(send1, recv1, 0, 0, 0, s1, r1.at[0])

    @pl.loop(1, ny)
    def _(k):
        load_tok(k).wait()
        project(0, k)
        send_part(send1, recv1, 0, k, 0, s1, r1.at[0])

    lru_loads[1].wait()

    @pl.loop(0, ny)
    def _(k):
        project(1, k)

    with jax.named_scope("perm"):
        build_perm()
    for copy in gate_loads + gel_loads:
        copy.wait()

    @pl.loop(0, ny)
    def _(k):
        gate_part(0, k)

    def got_all(ref, sem):
        remote(ref, ref, sem, sem, ctx=lax.rem(c + 1, n_ctx)).wait_recv()

    def sent_all(ref, sem):
        remote(ref, ref, sem, sem, ctx=lax.rem(c + 1, n_ctx)).wait_send()

    lanes_bs = bs // 128

    def wide(v):
        return jnp.concatenate([v] * lanes_bs, axis=-1)

    def conv_range(b, j0, nj):
        taps = conv_ref[:, b * bs : (b + 1) * bs].astype(F32)
        pos = wide(seg_b[pl.ds(j0, nj)])
        total = taps[0:1, :] * win[pl.ds(j0 + 3, nj)]
        for k in range(1, 4):
            total = total + taps[k : k + 1, :] * jnp.where(
                pos >= k, win[pl.ds(j0 + 3 - k, nj)], F32(0.0)
            )
        conv[pl.ds(pl.multiple_of(j0 * SUB, SUB * nj), nj * SUB), :] = total.reshape(nj * SUB, bs).astype(BF)

    def gates_range(b, r0, nr):
        grouped = conv[r0 : r0 + nr, :]
        lin_r[r0 : r0 + nr, :] = DOT(grouped, recw[b])
        lin_i[r0 : r0 + nr, :] = DOT(grouped, inpw[b])

    def scan_range(b, j0, nj, carry):
        cum, now = carry
        rows = pl.ds(pl.multiple_of(j0 * SUB, SUB * nj), nj * SUB)
        rate8 = 8.0 * rate_ref[:, b * bs : (b + 1) * bs]
        rate_gate = jax.nn.sigmoid(lin_r[rows, :])
        in_gate = jax.nn.sigmoid(lin_i[rows, :])
        fall = rate_gate * rate8
        starts = wide(seg_b[pl.ds(j0, nj)]).reshape(nj * SUB, bs) == 0
        step = jnp.where(starts, F32(0.0), jnp.exp(-fall))
        scale = jnp.where(starts, F32(1.0), jnp.sqrt(one_minus_exp_minus(2.0 * fall)))
        drive = scale * in_gate * conv[rows, :].astype(F32)
        for j in range(nj):
            a = step[j * SUB : (j + 1) * SUB]
            now = a * now + drive[j * SUB : (j + 1) * SUB]
            cum = a * cum
            decay[b, j0 + j] = cum
            state[b, j0 + j] = now
        return cum, now

    fresh = (jnp.ones((SUB, bs), F32), jnp.zeros((SUB, bs), F32))
    step_j = 8

    def first_pass(b, more):
        with jax.named_scope("wait1"):
            got_all(recv1.at[b, pl.ds(0, n_ctx - 1)], r1.at[b])
        got = recv1[b].reshape(rows_all, bs)
        quarter = rows_all // 4

        def permute(q):
            block = DOT(perm[q * quarter : (q + 1) * quarter, :], got)
            win[3 + q * quarter // SUB : 3 + (q + 1) * quarter // SUB] = block.reshape(quarter // SUB, SUB, bs)

        permute(3)
        tails = [win[seg_rows + k, SUB - 1 : SUB, :] for k in range(3)]
        rim_s[b] = jnp.concatenate(tails + [jnp.zeros((SUB - 3, bs), F32)], axis=0)

        @pl.when(c < n_ctx - 1)
        def _():
            remote(rim_s.at[b], rim_r.at[b], sr.at[b], rr.at[b], ctx=c + 1).start()

        for q in range(3):
            more(1)
            permute(q)
        more(1)

        @pl.loop(HEAD // step_j, seg_rows // step_j)
        def _(g):
            conv_range(b, g * step_j, step_j)

        body = rows_all - HEAD * SUB
        half = body // 2 // 16 * 16
        more(1)
        gates_range(b, HEAD * SUB, half)
        gates_range(b, HEAD * SUB + half, body - half)
        carry = fresh
        cuts = (HEAD // step_j, seg_rows // step_j // 2, seg_rows // step_j)
        for low, high in zip(cuts, cuts[1:]):
            more(2)
            carry = lax.fori_loop(
                low, high, lambda g, was: scan_range(b, g * step_j, step_j, was), carry
            )
        cum, now = carry
        more(2)
        ends[b, 2], ends[b, 3] = cum, now

    def second_pass(b):
        @pl.when(c == 0)
        def _():
            rim_r[b] = jnp.zeros((SUB, bs), F32)

        @pl.when(c > 0)
        def _():
            with jax.named_scope("waitrim"):
                got_all(rim_r.at[b], rr.at[b])

        for k in range(3):
            win[k] = jnp.concatenate(
                [rim_r[b, k : k + 1, :], win[seg_rows + k, 0 : SUB - 1, :]], axis=0
            )
        for g in range(HEAD // step_j):
            conv_range(b, g * step_j, step_j)
        gates_range(b, 0, HEAD * SUB)
        carry = fresh
        for g in range(HEAD // step_j):
            carry = scan_range(b, g * step_j, step_j, carry)
        ends[b, 0], ends[b, 1] = carry
        cum, now = carry[0] * ends[b, 2], ends[b, 2] * carry[1] + ends[b, 3]
        ends[b, 4], ends[b, 5] = cum, now
        whole_c, whole_h = cum[0:1], now[0:1]
        for s in range(1, SUB):
            whole_h = cum[s : s + 1] * whole_h + now[s : s + 1]
            whole_c = cum[s : s + 1] * whole_c
        sum_s[b] = jnp.concatenate([whole_c, whole_h], axis=0)

        @pl.loop(y + 1, ny)
        def _(to_y):
            for to_z in range(nz):
                remote(sum_s.at[b], sum_r.at[b, c], ss.at[b, to_y], rs.at[b, y], ctx=to_y * nz + to_z).start()

        @pl.loop(z + 1, nz)
        def _(to_z):
            remote(sum_s.at[b], sum_r.at[b, c], ss.at[b, ny + to_z], rs.at[b, ny + z], ctx=y * nz + to_z).start()

    def third_pass(b, send):
        def join(source, incoming):
            both = sum_r[b, source]
            return both[0:1] * incoming + both[1:2]

        def join_row(from_y, incoming):
            got_all(sum_r.at[b, pl.ds(from_y * nz, nz)], rs.at[b, from_y])
            for from_z in range(nz):
                incoming = join(from_y * nz + from_z, incoming)
            return incoming

        def join_own(from_z, incoming):
            got_all(sum_r.at[b, y * nz + from_z], rs.at[b, ny + from_z])
            return join(y * nz + from_z, incoming)

        with jax.named_scope("waitsum"):
            incoming = lax.fori_loop(0, y, join_row, jnp.zeros((1, bs), F32))
            incoming = lax.fori_loop(0, z, join_own, incoming)
        cum, now = ends[b, 4], ends[b, 5]
        lines = [incoming]
        for s in range(SUB - 1):
            lines.append(cum[s : s + 1] * lines[-1] + now[s : s + 1])
        head_in = jnp.concatenate(lines, axis=0)
        body_in = ends[b, 0] * head_in + ends[b, 1]

        def fix(g, into):
            j0 = g * step_j
            full = state[b, pl.ds(j0, step_j)] + decay[b, pl.ds(j0, step_j)] * into
            rows16[pl.ds(pl.multiple_of(j0 * SUB, step_j * SUB), step_j * SUB), :] = full.reshape(step_j * SUB, bs).astype(BF)
            return into

        for g in range(HEAD // step_j):
            fix(g, head_in)
        lax.fori_loop(HEAD // step_j, seg_rows // step_j, fix, body_in)

        @pl.loop(0, ny)
        def _(i):
            k = low(i + x, ny)
            block = DOT(perm_t[part_rows(k), :], rows16[...]).astype(BF)
            send2[b, pl.ds(low(y + k, ny) * nz, nz)] = block.reshape(nz, share, bs)
            if send:
                send_part(send2, recv2, b, i, x, s2, r2.at[b, group])

    def finish(b, first, last):
        @pl.loop(first, last)
        def _(i):
            other = low(y - i - x, ny)
            for q in range(per_y):
                owner = other * per_y + low(zg - q, per_y)

                @pl.when(owner == group)
                def _():
                    got_all(recv2.at[b, pl.ds(0, per_group - 1)], r2.at[b, owner])

                @pl.when(owner != group)
                def _():
                    got_all(recv2.at[b, pl.ds(0, per_group)], r2.at[b, owner])

                rows = pl.ds(pl.multiple_of(owner * mp_rows, mp_rows), mp_rows)
                got = recv2[b, pl.ds(owner * per_group, per_group)].reshape(mp_rows, bs)
                result = (got.astype(F32) * gate[b, rows, :]).astype(BF)

                @pl.when(owner == m)
                def _():
                    orecv[b, m] = result

                @pl.when(owner != m)
                def _():
                    fin[b, owner] = result
                    remote(fin.at[b, owner], orecv.at[b, m], sm.at[b], rm.at[b], mp=owner).start()

    scope = jax.named_scope
    more = pump(send1, recv1, 1, 0, w1, r1.at[1])
    with scope("sent0"):
        sent_all(send1.at[0, pl.ds(0, n_ctx - 1)], s1)
        more(window)
    with scope("gate1"):

        @pl.loop(0, ny // 2)
        def _(k):
            gate_part(1, k)

    with scope("first0"):
        first_pass(0, more)
    with scope("second0"):
        second_pass(0)
    with scope("more0"):
        more(n_ctx)
    with scope("gate1"):

        @pl.loop(ny // 2, ny)
        def _(k):
            gate_part(1, k)

    with scope("third0"):
        third_pass(0, False)
        more = pump(send2, recv2, 0, x, w2, r2.at[0, group])
        more(window)
    with scope("first1"):
        first_pass(1, more)
    with scope("second1"):
        second_pass(1)
    with scope("more1"):
        more(n_ctx)
    with scope("early0"):
        finish(0, 0, ny // 2)
    with scope("third1"):
        third_pass(1, True)

    with scope("finish0"):
        finish(0, ny // 2, ny)
    with scope("finish1"):
        finish(1, 0, ny)

    def out_copy(b, source):
        lane = pl.multiple_of(source * (blocks * bs) + b * bs, bs)
        return pltpu.make_async_copy(
            orecv.at[b, source], out_hbm.at[:, pl.ds(lane, bs)], out_sem.at[b, source]
        )

    with scope("drain"):
        window_end(send1, 1, 0, w1)
    window_end(send2, 0, x, w2)
    sent_all(send2.at[1, pl.ds(0, n_ctx - 1)], s2)
    for b in range(blocks):

        @pl.loop(y + 1, ny)
        def _(to_y):
            sent_all(sum_r.at[b, pl.ds(0, nz)], ss.at[b, to_y])

        @pl.loop(z + 1, nz)
        def _(to_z):
            sent_all(sum_s.at[b], ss.at[b, ny + to_z])

        @pl.when(c < n_ctx - 1)
        def _():
            sent_all(rim_s.at[b], sr.at[b])

        sent_all(fin.at[b, pl.ds(0, n_mp - 1)], sm.at[b])

    for b in range(blocks):
        with jax.named_scope("waitmp"):
            got_all(orecv.at[b, pl.ds(0, n_mp - 1)], rm.at[b])
        for source in range(n_mp):
            lane = source * (blocks * bs) + b * bs
            out_hbm[:, lane : lane + bs] = orecv[b, source]


def body(ny, nz, n_mp, tokens, lru_w, gelu_w, conv_w, recur_w, input_w, rate, seg, src):
    rows_all, depth = tokens.shape
    width = lru_w.shape[1]
    blocks, bs = recur_w.shape[:2]
    n_ctx = ny * nz
    share, seg_rows, mp_rows = rows_all // n_ctx, rows_all // SUB, rows_all // n_mp
    dma = pltpu.SemaphoreType.DMA
    return pl.pallas_call(
        functools.partial(kernel, (ny, nz, n_mp, blocks, bs)),
        out_shape=pltpu.VMEM((mp_rows, n_mp * width), BF),
        in_specs=[ANY, ANY, ANY, VMEM, ANY, ANY, VMEM, VMEM, VMEM],
        out_specs=VMEM,
        scratch_shapes=[
            pltpu.VMEM((rows_all, depth), BF),
            pltpu.VMEM((blocks, depth, bs), BF),
            pltpu.VMEM((blocks, depth, bs), BF),
            pltpu.VMEM((blocks, bs, bs), BF),
            pltpu.VMEM((blocks, bs, bs), BF),
            pltpu.VMEM((seg_rows, SUB, 128), jnp.int32),
            pltpu.VMEM((seg_rows, SUB, 128), jnp.int32),
            pltpu.VMEM((rows_all, rows_all), BF),
            pltpu.VMEM((rows_all, rows_all), BF),
            pltpu.VMEM((blocks, n_ctx, share, bs), BF),
            pltpu.VMEM((blocks, n_ctx, share, bs), BF),
            pltpu.VMEM((blocks, n_ctx, share, bs), BF),
            pltpu.VMEM((blocks, n_ctx, share, bs), BF),
            pltpu.VMEM((blocks, rows_all, bs), F32),
            pltpu.VMEM((blocks, n_mp, mp_rows, bs), BF),
            pltpu.VMEM((blocks, n_mp, mp_rows, bs), BF),
            pltpu.VMEM((seg_rows + 3, SUB, bs), F32),
            pltpu.VMEM((rows_all, bs), BF),
            pltpu.VMEM((rows_all, bs), F32),
            pltpu.VMEM((rows_all, bs), F32),
            pltpu.VMEM((blocks, seg_rows, SUB, bs), F32),
            pltpu.VMEM((blocks, seg_rows, SUB, bs), F32),
            pltpu.VMEM((blocks, 6, SUB, bs), F32),
            pltpu.VMEM((blocks, SUB, bs), F32),
            pltpu.VMEM((blocks, SUB, bs), F32),
            pltpu.VMEM((blocks, 2, bs), F32),
            pltpu.VMEM((blocks, n_ctx, 2, bs), F32),
            pltpu.VMEM((rows_all, bs), BF),
            dma((ny + 2 * blocks + 2,)),
            dma((blocks, n_mp)),
            dma,
            dma((blocks,)),
            dma((min(WINDOW, n_ctx // 2),)),
            dma,
            dma((blocks, n_mp)),
            dma((min(WINDOW, n_ctx // 2),)),
            dma((blocks,)),
            dma((blocks,)),
            dma((blocks, ny + nz)),
            dma((blocks, ny + nz)),
            dma((blocks,)),
            dma((blocks,)),
        ],
        compiler_params=pltpu.CompilerParams(
            collective_id=0, has_side_effects=True, vmem_limit_bytes=60 * 1024 * 1024
        ),
    )(
        tokens,
        lru_w,
        gelu_w,
        conv_w,
        recur_w,
        input_w,
        rate.reshape(1, width),
        seg.reshape(SUB, seg_rows),
        src.reshape(SUB, seg_rows),
    )


def solution(mesh, ny=None):
    n_ctx, n_mp = mesh.shape["ctx"], mesh.shape["mp"]
    ny = ny or 4
    in_specs = (
        P("ctx", None),
        P(None, "mp"),
        P(None, "mp"),
        P(None, "mp"),
        P("mp", None, None),
        P("mp", None, None),
        P("mp"),
        P("ctx"),
        P("ctx"),
    )
    out_specs = P(("ctx", "mp"), None)
    return jax.shard_map(
        functools.partial(body, ny, n_ctx // ny, n_mp),
        mesh=mesh,
        in_specs=in_specs,
        out_specs=out_specs,
        check_vma=False,
    )
```

```python
import functools

import jax
import jax.numpy as jnp
from jax import lax
from jax.experimental import pallas as pl
from jax.experimental.pallas import tpu as pltpu
from jax.sharding import PartitionSpec as P

MESH = pl.DeviceIdType.MESH
ANY = pl.BlockSpec(memory_space=pl.ANY)
VMEM = pl.BlockSpec(memory_space=pltpu.VMEM)
BF = jnp.bfloat16
F32 = jnp.float32
SUB = 8
HEAD = 16
DOT = functools.partial(jnp.dot, preferred_element_type=F32)


def one_minus_exp_minus(v):
    poly = F32(1.0 / 40320.0)
    for order in (5040.0, 720.0, 120.0, 24.0, 6.0, 2.0, 1.0):
        poly = F32(1.0 / order) - v * poly
    return v * poly


def kernel(
    dims,
    tok_hbm,
    lru_hbm,
    gelu_hbm,
    conv_ref,
    recur_hbm,
    input_hbm,
    rate_ref,
    seg_ref,
    src_ref,
    out,
    tok,
    lru,
    gel,
    recw,
    inpw,
    seg_b,
    idx_b,
    perm,
    perm_t,
    send1,
    recv1,
    send2,
    recv2,
    gate,
    fin,
    orecv,
    win,
    conv,
    lin_r,
    lin_i,
    decay,
    state,
    ends,
    rim_s,
    rim_r,
    sum_s,
    sum_r,
    rows16,
    load_sem,
    s1,
    r1,
    s2,
    r2,
    sm,
    rm,
    ss,
    rs,
    sr,
    rr,
):
    ny, nz, n_mp, blocks, bs = dims
    n_ctx = ny * nz
    half, most = n_ctx // 2, n_ctx * 3 // 4
    rows_all, depth = tok.shape
    share = rows_all // n_ctx
    part = rows_all // ny
    seg_rows = rows_all // SUB
    mp_rows = rows_all // n_mp
    per_y = n_mp // ny
    c = lax.axis_index("ctx")
    m = lax.axis_index("mp")
    y, z, x = c // nz, lax.rem(c, nz), m // 2

    def low(v, size):
        return v & (size - 1)

    def high(v, size):
        return lax.shift_right_logical(v, size.bit_length() - 1)

    barrier = pltpu.get_barrier_semaphore()

    for k in sorted(range(1, n_ctx), key=lambda k: -min(k // nz, ny - k // nz) - min(k % nz, nz - k % nz)):
        peer = low(y + k // nz, ny) * nz + low(z + k % nz, nz)
        pl.semaphore_signal(barrier, inc=1, device_id={"ctx": peer}, device_id_type=MESH)
    for k in range(1, n_mp):
        pl.semaphore_signal(
            barrier, inc=1, device_id={"mp": low(m + k, n_mp)}, device_id_type=MESH
        )

    def remote(src, dst, send_sem, recv_sem, **device):
        return pltpu.make_async_remote_copy(
            src_ref=src,
            dst_ref=dst,
            send_sem=send_sem,
            recv_sem=recv_sem,
            device_id=device,
            device_id_type=MESH,
        )

    def part_rows(k):
        return pl.ds(pl.multiple_of(low(y + k, ny) * part, part), part)

    def load_tok(k):
        return pltpu.make_async_copy(
            tok_hbm.at[part_rows(k)], tok.at[part_rows(k)], load_sem.at[k]
        )

    def load_w(hbm, buf, b, at):
        return pltpu.make_async_copy(
            hbm.at[:, b * bs : (b + 1) * bs], buf.at[b], load_sem.at[at]
        )

    at = ny
    lru_loads = [load_w(lru_hbm, lru, b, at + b) for b in range(blocks)]
    at += blocks
    gel_loads = [load_w(gelu_hbm, gel, b, at + b) for b in range(blocks)]
    at += blocks
    gate_loads = [
        pltpu.make_async_copy(recur_hbm, recw, load_sem.at[at]),
        pltpu.make_async_copy(input_hbm, inpw, load_sem.at[at + 1]),
    ]
    lru_loads[0].start()
    for k in range(ny):
        load_tok(k).start()
    for copy in lru_loads[1:] + gate_loads + gel_loads:
        copy.start()

    def project(b, k):
        rows = part_rows(k)
        branch = DOT(tok[rows, :], lru[b]).astype(BF)
        first = low(y + k, ny) * nz
        send1[b, pl.ds(first, nz)] = branch.reshape(nz, share, bs)

    per_group = mp_rows // share
    group = c // per_group
    zg = z // per_group

    def target(t, turn):
        to_y = low(y + high(t, nz) + turn, ny)
        to_g = low(zg + high(t, per_group), per_y)
        return to_y * nz + to_g * per_group + low(z + t, per_group)

    def send_one(buf, into, b, t, turn, s_sem, r_sem):
        d = target(t, turn)

        @pl.when(d != c)
        def _():
            remote(buf.at[b, d], into.at[b, c], s_sem, r_sem, ctx=d).start()

        @pl.when(d == c)
        def _():
            into[b, c] = buf[b, c]

    def send_part(buf, into, b, i, turn, s_sem, r_sem):
        for e in range(nz):
            send_one(buf, into, b, jnp.int32(i * nz + e), turn, s_sem, r_sem)

    def burst(buf, into, b, first, last, turn, s_sem, r_sem):
        @pl.loop(first, last)
        def _(t):
            send_one(buf, into, b, t, turn, s_sem, r_sem)

    def build_perm():
        src = src_ref[...]
        idx = (src // rows_all) * share + lax.rem(src, rows_all) - c * share
        seg = seg_ref[...]
        for j in range(seg_rows):
            idx_b[j] = jnp.broadcast_to(idx[:, j : j + 1], (SUB, 128))
            seg_b[j] = jnp.broadcast_to(seg[:, j : j + 1], (SUB, 128))
        lanes = lax.broadcasted_iota(jnp.int32, (128, 128), 1)

        @pl.loop(0, rows_all // 128)
        def _(g):
            want = idx_b[pl.ds(g * 16, 16)].reshape(128, 128)
            here = pl.ds(pl.multiple_of(g * 128, 128), 128)
            for t in range(rows_all // 128):
                hot = jnp.where(want == lanes + t * 128, F32(1.0), F32(0.0))
                perm[here, t * 128 : (t + 1) * 128] = hot.astype(BF)
                perm_t[t * 128 : (t + 1) * 128, here] = hot.T.astype(BF)

    def gate_part(b, k):
        rows = part_rows(k)
        line = DOT(tok[rows, :], gel[b]).astype(BF).astype(F32)
        gate[b, rows, :] = jax.nn.gelu(line, approximate=True)

    lru_loads[0].wait()
    load_tok(0).wait()
    project(0, 0)
    with jax.named_scope("barrier"):
        pl.semaphore_wait(barrier, n_ctx + n_mp - 2)
    send_part(send1, recv1, 0, 0, 0, s1.at[0], r1.at[0])

    @pl.loop(1, ny)
    def _(k):
        load_tok(k).wait()
        project(0, k)
        send_part(send1, recv1, 0, k, 0, s1.at[0], r1.at[0])

    lru_loads[1].wait()

    @pl.loop(0, ny)
    def _(k):
        project(1, k)

        @pl.when(k < ny // 2)
        def _():
            send_part(send1, recv1, 1, k, 0, s1.at[1], r1.at[1])

    with jax.named_scope("perm"):
        build_perm()
    for copy in gate_loads + gel_loads:
        copy.wait()

    @pl.loop(0, ny)
    def _(k):
        gate_part(0, k)

    def got_all(ref, sem):
        remote(ref, ref, sem, sem, ctx=lax.rem(c + 1, n_ctx)).wait_recv()

    def sent_all(ref, sem):
        remote(ref, ref, sem, sem, ctx=lax.rem(c + 1, n_ctx)).wait_send()

    lanes_bs = bs // 128

    def wide(v):
        return jnp.concatenate([v] * lanes_bs, axis=-1)

    def conv_range(b, j0, nj):
        taps = conv_ref[:, b * bs : (b + 1) * bs].astype(F32)
        pos = wide(seg_b[pl.ds(j0, nj)])
        total = taps[0:1, :] * win[b, pl.ds(j0 + 3, nj)]
        for k in range(1, 4):
            total = total + taps[k : k + 1, :] * jnp.where(
                pos >= k, win[b, pl.ds(j0 + 3 - k, nj)], F32(0.0)
            )
        conv[pl.ds(pl.multiple_of(j0 * SUB, SUB * nj), nj * SUB), :] = total.reshape(nj * SUB, bs).astype(BF)

    def gates_range(b, r0, nr):
        grouped = conv[r0 : r0 + nr, :]
        lin_r[r0 : r0 + nr, :] = DOT(grouped, recw[b])
        lin_i[r0 : r0 + nr, :] = DOT(grouped, inpw[b])

    def scan_range(b, j0, nj, carry):
        cum, now = carry
        rows = pl.ds(pl.multiple_of(j0 * SUB, SUB * nj), nj * SUB)
        rate8 = 8.0 * rate_ref[:, b * bs : (b + 1) * bs]
        rate_gate = jax.nn.sigmoid(lin_r[rows, :])
        in_gate = jax.nn.sigmoid(lin_i[rows, :])
        fall = rate_gate * rate8
        starts = wide(seg_b[pl.ds(j0, nj)]).reshape(nj * SUB, bs) == 0
        step = jnp.where(starts, F32(0.0), jnp.exp(-fall))
        scale = jnp.where(starts, F32(1.0), jnp.sqrt(one_minus_exp_minus(2.0 * fall)))
        drive = scale * in_gate * conv[rows, :].astype(F32)
        for j in range(nj):
            a = step[j * SUB : (j + 1) * SUB]
            now = a * now + drive[j * SUB : (j + 1) * SUB]
            cum = a * cum
            decay[b, j0 + j] = cum
            state[b, j0 + j] = now
        return cum, now

    fresh = (jnp.ones((SUB, bs), F32), jnp.zeros((SUB, bs), F32))
    step_j = 8

    quarter = rows_all // 4

    def permute(b, q):
        got = recv1[b].reshape(rows_all, bs)
        block = DOT(perm[q * quarter : (q + 1) * quarter, :], got)
        win[b, 3 + q * quarter // SUB : 3 + (q + 1) * quarter // SUB] = block.reshape(quarter // SUB, SUB, bs)

    def arrive(b):
        with jax.named_scope("wait1"):
            got_all(recv1.at[b, pl.ds(0, n_ctx - 1)], r1.at[b])
        permute(b, 3)
        tails = [win[b, seg_rows + k, SUB - 1 : SUB, :] for k in range(3)]
        rim_s[b] = jnp.concatenate(tails + [jnp.zeros((SUB - 3, bs), F32)], axis=0)

        @pl.when(c < n_ctx - 1)
        def _():
            remote(rim_s.at[b], rim_r.at[b], sr.at[b], rr.at[b], ctx=c + 1).start()

    def first_pass(b):
        for q in range(3):
            permute(b, q)

        @pl.loop(HEAD // step_j, seg_rows // step_j)
        def _(g):
            conv_range(b, g * step_j, step_j)

        size = rows_all - HEAD * SUB
        cut = size // 2 // 16 * 16
        gates_range(b, HEAD * SUB, cut)
        gates_range(b, HEAD * SUB + cut, size - cut)
        cum, now = lax.fori_loop(
            HEAD // step_j,
            seg_rows // step_j,
            lambda g, was: scan_range(b, g * step_j, step_j, was),
            fresh,
        )
        ends[b, 2], ends[b, 3] = cum, now

    def second_pass(b):
        @pl.when(c == 0)
        def _():
            rim_r[b] = jnp.zeros((SUB, bs), F32)

        @pl.when(c > 0)
        def _():
            with jax.named_scope("waitrim"):
                got_all(rim_r.at[b], rr.at[b])

        for k in range(3):
            win[b, k] = jnp.concatenate(
                [rim_r[b, k : k + 1, :], win[b, seg_rows + k, 0 : SUB - 1, :]], axis=0
            )
        for g in range(HEAD // step_j):
            conv_range(b, g * step_j, step_j)
        gates_range(b, 0, HEAD * SUB)
        carry = fresh
        for g in range(HEAD // step_j):
            carry = scan_range(b, g * step_j, step_j, carry)
        ends[b, 0], ends[b, 1] = carry
        cum, now = carry[0] * ends[b, 2], ends[b, 2] * carry[1] + ends[b, 3]
        ends[b, 4], ends[b, 5] = cum, now
        whole_c, whole_h = cum[0:1], now[0:1]
        for s in range(1, SUB):
            whole_h = cum[s : s + 1] * whole_h + now[s : s + 1]
            whole_c = cum[s : s + 1] * whole_c
        sum_s[b] = jnp.concatenate([whole_c, whole_h], axis=0)

        @pl.loop(y + 1, ny)
        def _(to_y):
            for to_z in range(nz):
                remote(sum_s.at[b], sum_r.at[b, c], ss.at[b, to_y], rs.at[b, y], ctx=to_y * nz + to_z).start()

        @pl.loop(z + 1, nz)
        def _(to_z):
            remote(sum_s.at[b], sum_r.at[b, c], ss.at[b, ny + to_z], rs.at[b, ny + z], ctx=y * nz + to_z).start()

    def third_pass(b, sends):
        def join(source, incoming):
            both = sum_r[b, source]
            return both[0:1] * incoming + both[1:2]

        def join_row(from_y, incoming):
            got_all(sum_r.at[b, pl.ds(from_y * nz, nz)], rs.at[b, from_y])
            for from_z in range(nz):
                incoming = join(from_y * nz + from_z, incoming)
            return incoming

        def join_own(from_z, incoming):
            got_all(sum_r.at[b, y * nz + from_z], rs.at[b, ny + from_z])
            return join(y * nz + from_z, incoming)

        with jax.named_scope("waitsum"):
            incoming = lax.fori_loop(0, y, join_row, jnp.zeros((1, bs), F32))
            incoming = lax.fori_loop(0, z, join_own, incoming)
        cum, now = ends[b, 4], ends[b, 5]
        lines = [incoming]
        for s in range(SUB - 1):
            lines.append(cum[s : s + 1] * lines[-1] + now[s : s + 1])
        head_in = jnp.concatenate(lines, axis=0)
        body_in = ends[b, 0] * head_in + ends[b, 1]

        def fix(g, into):
            j0 = g * step_j
            full = state[b, pl.ds(j0, step_j)] + decay[b, pl.ds(j0, step_j)] * into
            rows16[pl.ds(pl.multiple_of(j0 * SUB, step_j * SUB), step_j * SUB), :] = full.reshape(step_j * SUB, bs).astype(BF)
            return into

        for g in range(HEAD // step_j):
            fix(g, head_in)
        lax.fori_loop(HEAD // step_j, seg_rows // step_j, fix, body_in)

        @pl.loop(0, ny)
        def _(i):
            k = low(i + x, ny)
            block = DOT(perm_t[part_rows(k), :], rows16[...]).astype(BF)
            send2[b, pl.ds(low(y + k, ny) * nz, nz)] = block.reshape(nz, share, bs)
            @pl.when(i < sends)
            def _():
                send_part(send2, recv2, b, i, x, s2.at[b], r2.at[b, group])

    def finish(b, first, last):
        @pl.loop(first, last)
        def _(i):
            other = low(y - i - x, ny)
            for q in range(per_y):
                owner = other * per_y + low(zg - q, per_y)

                @pl.when(owner == group)
                def _():
                    got_all(recv2.at[b, pl.ds(0, per_group - 1)], r2.at[b, owner])

                @pl.when(owner != group)
                def _():
                    got_all(recv2.at[b, pl.ds(0, per_group)], r2.at[b, owner])

                rows = pl.ds(pl.multiple_of(owner * mp_rows, mp_rows), mp_rows)
                got = recv2[b, pl.ds(owner * per_group, per_group)].reshape(mp_rows, bs)
                result = (got.astype(F32) * gate[b, rows, :]).astype(BF)

                @pl.when(owner == m)
                def _():
                    orecv[b, m] = result

                @pl.when(owner != m)
                def _():
                    fin[b, owner] = result
                    remote(fin.at[b, owner], orecv.at[b, m], sm.at[b], rm.at[b], mp=owner).start()

    scope = jax.named_scope
    with scope("gate1"):

        @pl.loop(0, ny // 2)
        def _(k):
            gate_part(1, k)

    with scope("arrive0"):
        arrive(0)
    burst(send1, recv1, 1, half, most, 0, s1.at[1], r1.at[1])
    with scope("first0"):
        first_pass(0)
    with scope("second0"):
        second_pass(0)
    burst(send1, recv1, 1, most, n_ctx, 0, s1.at[1], r1.at[1])
    with scope("gate1"):

        @pl.loop(ny // 2, ny)
        def _(k):
            gate_part(1, k)

    with scope("third0"):
        third_pass(0, ny // 2)
    with scope("arrive1"):
        arrive(1)
    with scope("first1"):
        first_pass(1)
    with scope("second1"):
        second_pass(1)
    burst(send2, recv2, 0, half, n_ctx, x, s2.at[0], r2.at[0, group])
    with scope("early0"):
        finish(0, 0, ny // 2)
    with scope("third1"):
        third_pass(1, ny)
    with scope("finish0"):
        finish(0, ny // 2, ny)
    with scope("finish1"):
        finish(1, 0, ny)

    for b in range(blocks):
        sent_all(send1.at[b, pl.ds(0, n_ctx - 1)], s1.at[b])
        sent_all(send2.at[b, pl.ds(0, n_ctx - 1)], s2.at[b])
    for b in range(blocks):

        @pl.loop(y + 1, ny)
        def _(to_y):
            sent_all(sum_r.at[b, pl.ds(0, nz)], ss.at[b, to_y])

        @pl.loop(z + 1, nz)
        def _(to_z):
            sent_all(sum_s.at[b], ss.at[b, ny + to_z])

        @pl.when(c < n_ctx - 1)
        def _():
            sent_all(rim_s.at[b], sr.at[b])

        sent_all(fin.at[b, pl.ds(0, n_mp - 1)], sm.at[b])

    for b in range(blocks):
        with jax.named_scope("waitmp"):
            got_all(orecv.at[b, pl.ds(0, n_mp - 1)], rm.at[b])
        for source in range(n_mp):
            lane = source * (blocks * bs) + b * bs
            out[:, lane : lane + bs] = orecv[b, source]


def body(ny, nz, n_mp, tokens, lru_w, gelu_w, conv_w, recur_w, input_w, rate, seg, src):
    rows_all, depth = tokens.shape
    width = lru_w.shape[1]
    blocks, bs = recur_w.shape[:2]
    n_ctx = ny * nz
    share, seg_rows, mp_rows = rows_all // n_ctx, rows_all // SUB, rows_all // n_mp
    dma = pltpu.SemaphoreType.DMA
    return pl.pallas_call(
        functools.partial(kernel, (ny, nz, n_mp, blocks, bs)),
        out_shape=pltpu.VMEM((mp_rows, n_mp * width), BF),
        in_specs=[ANY, ANY, ANY, VMEM, ANY, ANY, VMEM, VMEM, VMEM],
        out_specs=VMEM,
        scratch_shapes=[
            pltpu.VMEM((rows_all, depth), BF),
            pltpu.VMEM((blocks, depth, bs), BF),
            pltpu.VMEM((blocks, depth, bs), BF),
            pltpu.VMEM((blocks, bs, bs), BF),
            pltpu.VMEM((blocks, bs, bs), BF),
            pltpu.VMEM((seg_rows, SUB, 128), jnp.int32),
            pltpu.VMEM((seg_rows, SUB, 128), jnp.int32),
            pltpu.VMEM((rows_all, rows_all), BF),
            pltpu.VMEM((rows_all, rows_all), BF),
            pltpu.VMEM((blocks, n_ctx, share, bs), BF),
            pltpu.VMEM((blocks, n_ctx, share, bs), BF),
            pltpu.VMEM((blocks, n_ctx, share, bs), BF),
            pltpu.VMEM((blocks, n_ctx, share, bs), BF),
            pltpu.VMEM((blocks, rows_all, bs), F32),
            pltpu.VMEM((blocks, n_mp, mp_rows, bs), BF),
            pltpu.VMEM((blocks, n_mp, mp_rows, bs), BF),
            pltpu.VMEM((blocks, seg_rows + 3, SUB, bs), F32),
            pltpu.VMEM((rows_all, bs), BF),
            pltpu.VMEM((rows_all, bs), F32),
            pltpu.VMEM((rows_all, bs), F32),
            pltpu.VMEM((blocks, seg_rows, SUB, bs), F32),
            pltpu.VMEM((blocks, seg_rows, SUB, bs), F32),
            pltpu.VMEM((blocks, 6, SUB, bs), F32),
            pltpu.VMEM((blocks, SUB, bs), F32),
            pltpu.VMEM((blocks, SUB, bs), F32),
            pltpu.VMEM((blocks, 2, bs), F32),
            pltpu.VMEM((blocks, n_ctx, 2, bs), F32),
            pltpu.VMEM((rows_all, bs), BF),
            dma((ny + 2 * blocks + 2,)),
            dma((blocks,)),
            dma((blocks,)),
            dma((blocks,)),
            dma((blocks, n_mp)),
            dma((blocks,)),
            dma((blocks,)),
            dma((blocks, ny + nz)),
            dma((blocks, ny + nz)),
            dma((blocks,)),
            dma((blocks,)),
        ],
        compiler_params=pltpu.CompilerParams(
            collective_id=0, has_side_effects=True, vmem_limit_bytes=60 * 1024 * 1024
        ),
    )(
        tokens,
        lru_w,
        gelu_w,
        conv_w,
        recur_w,
        input_w,
        rate.reshape(1, width),
        seg.reshape(SUB, seg_rows),
        src.reshape(SUB, seg_rows),
    )


def solution(mesh, ny=None):
    n_ctx, n_mp = mesh.shape["ctx"], mesh.shape["mp"]
    ny = ny or 4
    in_specs = (
        P("ctx", None),
        P(None, "mp"),
        P(None, "mp"),
        P(None, "mp"),
        P("mp", None, None),
        P("mp", None, None),
        P("mp"),
        P("ctx"),
        P("ctx"),
    )
    out_specs = P(("ctx", "mp"), None)
    return jax.shard_map(
        functools.partial(body, ny, n_ctx // ny, n_mp),
        mesh=mesh,
        in_specs=in_specs,
        out_specs=out_specs,
        check_vma=False,
    )
```

```python
import functools

import jax
import jax.numpy as jnp
from jax import lax
from jax.experimental import pallas as pl
from jax.experimental.pallas import tpu as pltpu
from jax.sharding import PartitionSpec as P

MESH = pl.DeviceIdType.MESH
ANY = pl.BlockSpec(memory_space=pl.ANY)
VMEM = pl.BlockSpec(memory_space=pltpu.VMEM)
BF = jnp.bfloat16
F32 = jnp.float32
SUB = 8
HEAD = 16
DOT = functools.partial(jnp.dot, preferred_element_type=F32)


def one_minus_exp_minus(v):
    poly = F32(1.0 / 40320.0)
    for order in (5040.0, 720.0, 120.0, 24.0, 6.0, 2.0, 1.0):
        poly = F32(1.0 / order) - v * poly
    return v * poly


def kernel(
    dims,
    tok_hbm,
    lru_hbm,
    gelu_hbm,
    conv_ref,
    recur_hbm,
    input_hbm,
    rate_ref,
    seg_ref,
    src_ref,
    out,
    tok,
    lru,
    gel,
    recw,
    inpw,
    seg_b,
    idx_b,
    perm,
    perm_t,
    send1,
    recv1,
    send2,
    recv2,
    gate,
    fin,
    orecv,
    win,
    conv,
    lin_r,
    lin_i,
    decay,
    state,
    ends,
    rim_s,
    rim_r,
    sum_s,
    sum_r,
    rows16,
    load_sem,
    s1,
    r1,
    s2,
    r2,
    sm,
    rm,
    ss,
    rs,
    sr,
    rr,
):
    ny, nz, n_mp, blocks, bs = dims
    n_ctx = ny * nz
    half, most = n_ctx // 2, n_ctx * 3 // 4
    rows_all, depth = tok.shape
    share = rows_all // n_ctx
    part = rows_all // ny
    seg_rows = rows_all // SUB
    mp_rows = rows_all // n_mp
    per_y = n_mp // ny
    c = lax.axis_index("ctx")
    m = lax.axis_index("mp")
    y, z, x = c // nz, lax.rem(c, nz), m // 2

    def low(v, size):
        return v & (size - 1)

    def high(v, size):
        return lax.shift_right_logical(v, size.bit_length() - 1)

    barrier = pltpu.get_barrier_semaphore()

    for k in sorted(range(1, n_ctx), key=lambda k: -min(k // nz, ny - k // nz) - min(k % nz, nz - k % nz)):
        peer = low(y + k // nz, ny) * nz + low(z + k % nz, nz)
        pl.semaphore_signal(barrier, inc=1, device_id={"ctx": peer}, device_id_type=MESH)
    for k in range(1, n_mp):
        pl.semaphore_signal(
            barrier, inc=1, device_id={"mp": low(m + k, n_mp)}, device_id_type=MESH
        )

    def remote(src, dst, send_sem, recv_sem, **device):
        return pltpu.make_async_remote_copy(
            src_ref=src,
            dst_ref=dst,
            send_sem=send_sem,
            recv_sem=recv_sem,
            device_id=device,
            device_id_type=MESH,
        )

    def part_rows(k):
        return pl.ds(pl.multiple_of(low(y + k, ny) * part, part), part)

    def load_tok(k):
        return pltpu.make_async_copy(
            tok_hbm.at[part_rows(k)], tok.at[part_rows(k)], load_sem.at[k]
        )

    def load_w(hbm, buf, b, at):
        return pltpu.make_async_copy(
            hbm.at[:, b * bs : (b + 1) * bs], buf.at[b], load_sem.at[at]
        )

    at = ny
    lru_loads = [load_w(lru_hbm, lru, b, at + b) for b in range(blocks)]
    at += blocks
    gel_loads = [load_w(gelu_hbm, gel, b, at + b) for b in range(blocks)]
    at += blocks
    gate_loads = [
        pltpu.make_async_copy(recur_hbm, recw, load_sem.at[at]),
        pltpu.make_async_copy(input_hbm, inpw, load_sem.at[at + 1]),
    ]
    lru_loads[0].start()
    for k in range(ny):
        load_tok(k).start()
    for copy in lru_loads[1:] + gate_loads + gel_loads:
        copy.start()

    def project(b, k):
        rows = part_rows(k)
        branch = DOT(tok[rows, :], lru[b]).astype(BF)
        first = low(y + k, ny) * nz
        send1[b, pl.ds(first, nz)] = branch.reshape(nz, share, bs)

    per_group = mp_rows // share
    group = c // per_group
    zg = z // per_group

    def target(t, turn):
        to_y = low(y + high(t, nz) + turn, ny)
        to_g = low(zg + high(t, per_group), per_y)
        return to_y * nz + to_g * per_group + low(z + t, per_group)

    def send_one(buf, into, b, t, turn, s_sem, r_sem):
        d = target(t, turn)

        @pl.when(d != c)
        def _():
            remote(buf.at[b, d], into.at[b, c], s_sem, r_sem, ctx=d).start()

        @pl.when(d == c)
        def _():
            into[b, c] = buf[b, c]

    def send_part(buf, into, b, i, turn, s_sem, r_sem):
        for e in range(nz):
            send_one(buf, into, b, jnp.int32(i * nz + e), turn, s_sem, r_sem)

    def burst(buf, into, b, first, last, turn, s_sem, r_sem):
        @pl.loop(first, last)
        def _(t):
            send_one(buf, into, b, t, turn, s_sem, r_sem)

    def build_perm():
        src = src_ref[...]
        idx = (src // rows_all) * share + lax.rem(src, rows_all) - c * share
        seg = seg_ref[...]
        for j in range(seg_rows):
            idx_b[j] = jnp.broadcast_to(idx[:, j : j + 1], (SUB, 128))
            seg_b[j] = jnp.broadcast_to(seg[:, j : j + 1], (SUB, 128))
        lanes = lax.broadcasted_iota(jnp.int32, (128, 128), 1)

        @pl.loop(0, rows_all // 128)
        def _(g):
            want = idx_b[pl.ds(g * 16, 16)].reshape(128, 128)
            here = pl.ds(pl.multiple_of(g * 128, 128), 128)
            for t in range(rows_all // 128):
                hot = jnp.where(want == lanes + t * 128, F32(1.0), F32(0.0))
                perm[here, t * 128 : (t + 1) * 128] = hot.astype(BF)
                perm_t[t * 128 : (t + 1) * 128, here] = hot.T.astype(BF)

    def gate_part(b, k):
        rows = part_rows(k)
        line = DOT(tok[rows, :], gel[b]).astype(BF).astype(F32)
        gate[b, rows, :] = jax.nn.gelu(line, approximate=True)

    lru_loads[0].wait()
    load_tok(0).wait()
    project(0, 0)
    with jax.named_scope("barrier"):
        pl.semaphore_wait(barrier, n_ctx + n_mp - 2)
    send_part(send1, recv1, 0, 0, 0, s1.at[0], r1.at[0])

    @pl.loop(1, ny)
    def _(k):
        load_tok(k).wait()
        project(0, k)
        send_part(send1, recv1, 0, k, 0, s1.at[0], r1.at[0])

    lru_loads[1].wait()

    @pl.loop(0, ny)
    def _(k):
        project(1, k)

        @pl.when(k < ny // 2)
        def _():
            send_part(send1, recv1, 1, k, 0, s1.at[1], r1.at[1])

    with jax.named_scope("perm"):
        build_perm()
    for copy in gate_loads + gel_loads:
        copy.wait()

    @pl.loop(0, ny)
    def _(k):
        gate_part(0, k)

    def got_all(ref, sem):
        remote(ref, ref, sem, sem, ctx=lax.rem(c + 1, n_ctx)).wait_recv()

    def sent_all(ref, sem):
        remote(ref, ref, sem, sem, ctx=lax.rem(c + 1, n_ctx)).wait_send()

    lanes_bs = bs // 128

    def wide(v):
        return jnp.concatenate([v] * lanes_bs, axis=-1)

    def conv_range(b, j0, nj):
        taps = conv_ref[:, b * bs : (b + 1) * bs].astype(F32)
        pos = wide(seg_b[pl.ds(j0, nj)])
        total = taps[0:1, :] * win[b, pl.ds(j0 + 3, nj)]
        for k in range(1, 4):
            total = total + taps[k : k + 1, :] * jnp.where(
                pos >= k, win[b, pl.ds(j0 + 3 - k, nj)], F32(0.0)
            )
        conv[pl.ds(pl.multiple_of(j0 * SUB, SUB * nj), nj * SUB), :] = total.reshape(nj * SUB, bs).astype(BF)

    def gates_range(b, r0, nr):
        grouped = conv[r0 : r0 + nr, :]
        lin_r[r0 : r0 + nr, :] = DOT(grouped, recw[b])
        lin_i[r0 : r0 + nr, :] = DOT(grouped, inpw[b])

    def scan_range(b, j0, nj, carry):
        cum, now = carry
        rows = pl.ds(pl.multiple_of(j0 * SUB, SUB * nj), nj * SUB)
        rate8 = 8.0 * rate_ref[:, b * bs : (b + 1) * bs]
        rate_gate = jax.nn.sigmoid(lin_r[rows, :])
        in_gate = jax.nn.sigmoid(lin_i[rows, :])
        fall = rate_gate * rate8
        starts = wide(seg_b[pl.ds(j0, nj)]).reshape(nj * SUB, bs) == 0
        step = jnp.where(starts, F32(0.0), jnp.exp(-fall))
        scale = jnp.where(starts, F32(1.0), jnp.sqrt(one_minus_exp_minus(2.0 * fall)))
        drive = scale * in_gate * conv[rows, :].astype(F32)
        for j in range(nj):
            a = step[j * SUB : (j + 1) * SUB]
            now = a * now + drive[j * SUB : (j + 1) * SUB]
            cum = a * cum
            decay[b, j0 + j] = cum
            state[b, j0 + j] = now
        return cum, now

    fresh = (jnp.ones((SUB, bs), F32), jnp.zeros((SUB, bs), F32))
    step_j = 16

    quarter = rows_all // 4

    def permute(b, q):
        got = recv1[b].reshape(rows_all, bs)
        block = DOT(perm[q * quarter : (q + 1) * quarter, :], got)
        win[b, 3 + q * quarter // SUB : 3 + (q + 1) * quarter // SUB] = block.reshape(quarter // SUB, SUB, bs)

    def arrive(b):
        with jax.named_scope("wait1"):
            got_all(recv1.at[b, pl.ds(0, n_ctx - 1)], r1.at[b])
        permute(b, 3)
        tails = [win[b, seg_rows + k, SUB - 1 : SUB, :] for k in range(3)]
        rim_s[b] = jnp.concatenate(tails + [jnp.zeros((SUB - 3, bs), F32)], axis=0)

        @pl.when(c < n_ctx - 1)
        def _():
            remote(rim_s.at[b], rim_r.at[b], sr.at[b], rr.at[b], ctx=c + 1).start()

    def first_pass(b):
        for q in range(3):
            permute(b, q)

        @pl.loop(HEAD // step_j, seg_rows // step_j)
        def _(g):
            conv_range(b, g * step_j, step_j)

        size = rows_all - HEAD * SUB
        cut = size // 2 // 16 * 16
        gates_range(b, HEAD * SUB, cut)
        gates_range(b, HEAD * SUB + cut, size - cut)
        cum, now = lax.fori_loop(
            HEAD // step_j,
            seg_rows // step_j,
            lambda g, was: scan_range(b, g * step_j, step_j, was),
            fresh,
        )
        ends[b, 2], ends[b, 3] = cum, now

    def second_pass(b):
        @pl.when(c == 0)
        def _():
            rim_r[b] = jnp.zeros((SUB, bs), F32)

        @pl.when(c > 0)
        def _():
            with jax.named_scope("waitrim"):
                got_all(rim_r.at[b], rr.at[b])

        for k in range(3):
            win[b, k] = jnp.concatenate(
                [rim_r[b, k : k + 1, :], win[b, seg_rows + k, 0 : SUB - 1, :]], axis=0
            )
        for g in range(HEAD // step_j):
            conv_range(b, g * step_j, step_j)
        gates_range(b, 0, HEAD * SUB)
        carry = fresh
        for g in range(HEAD // step_j):
            carry = scan_range(b, g * step_j, step_j, carry)
        ends[b, 0], ends[b, 1] = carry
        cum, now = carry[0] * ends[b, 2], ends[b, 2] * carry[1] + ends[b, 3]
        ends[b, 4], ends[b, 5] = cum, now
        whole_c, whole_h = cum[0:1], now[0:1]
        for s in range(1, SUB):
            whole_h = cum[s : s + 1] * whole_h + now[s : s + 1]
            whole_c = cum[s : s + 1] * whole_c
        sum_s[b] = jnp.concatenate([whole_c, whole_h], axis=0)

        @pl.loop(y + 1, ny)
        def _(to_y):
            for to_z in range(nz):
                remote(sum_s.at[b], sum_r.at[b, c], ss.at[b, to_y], rs.at[b, y], ctx=to_y * nz + to_z).start()

        @pl.loop(z + 1, nz)
        def _(to_z):
            remote(sum_s.at[b], sum_r.at[b, c], ss.at[b, ny + to_z], rs.at[b, ny + z], ctx=y * nz + to_z).start()

    def third_pass(b, sends):
        def join(source, incoming):
            both = sum_r[b, source]
            return both[0:1] * incoming + both[1:2]

        def join_row(from_y, incoming):
            got_all(sum_r.at[b, pl.ds(from_y * nz, nz)], rs.at[b, from_y])
            for from_z in range(nz):
                incoming = join(from_y * nz + from_z, incoming)
            return incoming

        def join_own(from_z, incoming):
            got_all(sum_r.at[b, y * nz + from_z], rs.at[b, ny + from_z])
            return join(y * nz + from_z, incoming)

        with jax.named_scope("waitsum"):
            incoming = lax.fori_loop(0, y, join_row, jnp.zeros((1, bs), F32))
            incoming = lax.fori_loop(0, z, join_own, incoming)
        cum, now = ends[b, 4], ends[b, 5]
        lines = [incoming]
        for s in range(SUB - 1):
            lines.append(cum[s : s + 1] * lines[-1] + now[s : s + 1])
        head_in = jnp.concatenate(lines, axis=0)
        body_in = ends[b, 0] * head_in + ends[b, 1]

        def fix(g, into):
            j0 = g * step_j
            full = state[b, pl.ds(j0, step_j)] + decay[b, pl.ds(j0, step_j)] * into
            rows16[pl.ds(pl.multiple_of(j0 * SUB, step_j * SUB), step_j * SUB), :] = full.reshape(step_j * SUB, bs).astype(BF)
            return into

        for g in range(HEAD // step_j):
            fix(g, head_in)
        lax.fori_loop(HEAD // step_j, seg_rows // step_j, fix, body_in)

        @pl.loop(0, ny)
        def _(i):
            k = low(i + x, ny)
            block = DOT(perm_t[part_rows(k), :], rows16[...]).astype(BF)
            send2[b, pl.ds(low(y + k, ny) * nz, nz)] = block.reshape(nz, share, bs)
            @pl.when(i < sends)
            def _():
                send_part(send2, recv2, b, i, x, s2.at[b], r2.at[b, group])

    def finish(b, first, last):
        @pl.loop(first, last)
        def _(i):
            other = low(y - i - x, ny)
            for q in range(per_y):
                owner = other * per_y + low(zg - q, per_y)

                @pl.when(owner == group)
                def _():
                    got_all(recv2.at[b, pl.ds(0, per_group - 1)], r2.at[b, owner])

                @pl.when(owner != group)
                def _():
                    got_all(recv2.at[b, pl.ds(0, per_group)], r2.at[b, owner])

                rows = pl.ds(pl.multiple_of(owner * mp_rows, mp_rows), mp_rows)
                got = recv2[b, pl.ds(owner * per_group, per_group)].reshape(mp_rows, bs)
                result = (got.astype(F32) * gate[b, rows, :]).astype(BF)

                @pl.when(owner == m)
                def _():
                    orecv[b, m] = result

                @pl.when(owner != m)
                def _():
                    fin[b, owner] = result
                    remote(fin.at[b, owner], orecv.at[b, m], sm.at[b], rm.at[b], mp=owner).start()

    scope = jax.named_scope
    with scope("gate1"):

        @pl.loop(0, ny // 2)
        def _(k):
            gate_part(1, k)

    with scope("arrive0"):
        arrive(0)
    burst(send1, recv1, 1, half, most, 0, s1.at[1], r1.at[1])
    with scope("first0"):
        first_pass(0)
    with scope("second0"):
        second_pass(0)
    burst(send1, recv1, 1, most, n_ctx, 0, s1.at[1], r1.at[1])
    with scope("gate1"):

        @pl.loop(ny // 2, ny)
        def _(k):
            gate_part(1, k)

    with scope("third0"):
        third_pass(0, ny // 2)
    with scope("arrive1"):
        arrive(1)
    with scope("first1"):
        first_pass(1)
    with scope("second1"):
        second_pass(1)
    burst(send2, recv2, 0, half, n_ctx, x, s2.at[0], r2.at[0, group])
    with scope("early0"):
        finish(0, 0, ny // 2)
    with scope("third1"):
        third_pass(1, ny)
    with scope("finish0"):
        finish(0, ny // 2, ny)
    with scope("finish1"):
        finish(1, 0, ny)

    for b in range(blocks):
        sent_all(send1.at[b, pl.ds(0, n_ctx - 1)], s1.at[b])
        sent_all(send2.at[b, pl.ds(0, n_ctx - 1)], s2.at[b])
    for b in range(blocks):

        @pl.loop(y + 1, ny)
        def _(to_y):
            sent_all(sum_r.at[b, pl.ds(0, nz)], ss.at[b, to_y])

        @pl.loop(z + 1, nz)
        def _(to_z):
            sent_all(sum_s.at[b], ss.at[b, ny + to_z])

        @pl.when(c < n_ctx - 1)
        def _():
            sent_all(rim_s.at[b], sr.at[b])

        sent_all(fin.at[b, pl.ds(0, n_mp - 1)], sm.at[b])

    for b in range(blocks):
        with jax.named_scope("waitmp"):
            got_all(orecv.at[b, pl.ds(0, n_mp - 1)], rm.at[b])
        for source in range(n_mp):
            lane = source * (blocks * bs) + b * bs
            out[:, lane : lane + bs] = orecv[b, source]


def body(ny, nz, n_mp, tokens, lru_w, gelu_w, conv_w, recur_w, input_w, rate, seg, src):
    rows_all, depth = tokens.shape
    width = lru_w.shape[1]
    blocks, bs = recur_w.shape[:2]
    n_ctx = ny * nz
    share, seg_rows, mp_rows = rows_all // n_ctx, rows_all // SUB, rows_all // n_mp
    dma = pltpu.SemaphoreType.DMA
    return pl.pallas_call(
        functools.partial(kernel, (ny, nz, n_mp, blocks, bs)),
        out_shape=pltpu.VMEM((mp_rows, n_mp * width), BF),
        in_specs=[ANY, ANY, ANY, VMEM, ANY, ANY, VMEM, VMEM, VMEM],
        out_specs=VMEM,
        scratch_shapes=[
            pltpu.VMEM((rows_all, depth), BF),
            pltpu.VMEM((blocks, depth, bs), BF),
            pltpu.VMEM((blocks, depth, bs), BF),
            pltpu.VMEM((blocks, bs, bs), BF),
            pltpu.VMEM((blocks, bs, bs), BF),
            pltpu.VMEM((seg_rows, SUB, 128), jnp.int32),
            pltpu.VMEM((seg_rows, SUB, 128), jnp.int32),
            pltpu.VMEM((rows_all, rows_all), BF),
            pltpu.VMEM((rows_all, rows_all), BF),
            pltpu.VMEM((blocks, n_ctx, share, bs), BF),
            pltpu.VMEM((blocks, n_ctx, share, bs), BF),
            pltpu.VMEM((blocks, n_ctx, share, bs), BF),
            pltpu.VMEM((blocks, n_ctx, share, bs), BF),
            pltpu.VMEM((blocks, rows_all, bs), F32),
            pltpu.VMEM((blocks, n_mp, mp_rows, bs), BF),
            pltpu.VMEM((blocks, n_mp, mp_rows, bs), BF),
            pltpu.VMEM((blocks, seg_rows + 3, SUB, bs), F32),
            pltpu.VMEM((rows_all, bs), BF),
            pltpu.VMEM((rows_all, bs), F32),
            pltpu.VMEM((rows_all, bs), F32),
            pltpu.VMEM((blocks, seg_rows, SUB, bs), F32),
            pltpu.VMEM((blocks, seg_rows, SUB, bs), F32),
            pltpu.VMEM((blocks, 6, SUB, bs), F32),
            pltpu.VMEM((blocks, SUB, bs), F32),
            pltpu.VMEM((blocks, SUB, bs), F32),
            pltpu.VMEM((blocks, 2, bs), F32),
            pltpu.VMEM((blocks, n_ctx, 2, bs), F32),
            pltpu.VMEM((rows_all, bs), BF),
            dma((ny + 2 * blocks + 2,)),
            dma((blocks,)),
            dma((blocks,)),
            dma((blocks,)),
            dma((blocks, n_mp)),
            dma((blocks,)),
            dma((blocks,)),
            dma((blocks, ny + nz)),
            dma((blocks, ny + nz)),
            dma((blocks,)),
            dma((blocks,)),
        ],
        compiler_params=pltpu.CompilerParams(
            collective_id=0, has_side_effects=True, vmem_limit_bytes=60 * 1024 * 1024
        ),
    )(
        tokens,
        lru_w,
        gelu_w,
        conv_w,
        recur_w,
        input_w,
        rate.reshape(1, width),
        seg.reshape(SUB, seg_rows),
        src.reshape(SUB, seg_rows),
    )


def solution(mesh, ny=None):
    n_ctx, n_mp = mesh.shape["ctx"], mesh.shape["mp"]
    ny = ny or 4
    in_specs = (
        P("ctx", None),
        P(None, "mp"),
        P(None, "mp"),
        P(None, "mp"),
        P("mp", None, None),
        P("mp", None, None),
        P("mp"),
        P("ctx"),
        P("ctx"),
    )
    out_specs = P(("ctx", "mp"), None)
    return jax.shard_map(
        functools.partial(body, ny, n_ctx // ny, n_mp),
        mesh=mesh,
        in_specs=in_specs,
        out_specs=out_specs,
        check_vma=False,
    )
```
